32 devices in a mesh: exp: 8 (over y, x, core), tp: 4 (over z).
Axes of the slice: x: 2, y: 2, z: 4, core: 2. Of those that a mesh axis runs over, the one named last changes fastest.
Arguments:
- attn_part: bfloat16 [4, 256, 7168], P('tp', 'exp'), may hold values from -2.5 to 2.5
- resid: bfloat16 [256, 7168], P('exp', 'tp'), may hold values from -50 to 50
- refusal: float32 [7168], replicated, may hold values from -4 to 4
- norm_gain: float32 [7168], P('tp'), may hold values from 0.5 to 1.5
- route_ids: int32 [256, 8], P('exp'), may hold values from 0 to 31, all different within a row; in each aligned block of 32 rows (0 to 31, 32 to 63, ...) at most 16 rows name the same one
- gate_q: int32 [256, 8], P('exp'), may hold values from 16 to 255
- w_gate: bfloat16 [32, 7168, 2048], P('exp', None, 'tp'), may hold values from -0.0625 to 0.0625
- w_up: bfloat16 [32, 7168, 2048], P('exp', None, 'tp'), may hold values from -0.0625 to 0.0625
- w_down: bfloat16 [32, 2048, 7168], P('exp', 'tp'), may hold values from -0.125 to 0.125
Outputs:
- layer_out: bfloat16 [256, 7168], P('exp', 'tp')
The draws below stay inside these ranges and needn't reach their ends.
Inputs may be any that keep to these rules, and one draw needn't show every extreme that they name: `route_ids`: each row names 8 different experts; in each aligned block of 32 rows (the tokens of one index of exp) no expert is named by more than 16 rows, a bound that some block reaches.
All inputs are finite; a program needn't handle non-finite values.
Results may differ from the reference program's by a relative error of at most 0.015.
Values may be sent and summed in bfloat16 or wider, within the bound.
No kernel may reach another device: no remote copies, remote signals or barrier semaphores. Data moves between devices by JAX's collectives and lax.ppermute only.
A program may use at most 256 MiB of HBM per device.

```python
import math
import jax
import jax.numpy as jnp
import numpy as np
from jax import lax

D = 7168
H = 2048
TOP = 8
TOK_GRP = 32
HG = 4
EXPERTS = 32
CAP = 16
TOKENS = 256
N_EXP = 8
N_TP = 4


def direction_base(key):
    return jnp.clip(jax.random.normal(jax.random.fold_in(key, 7), (D,), jnp.float32), -4.0, 4.0)


def draw_refusal(key, part):
    return direction_base(key)


def draw_resid(key, part):
    base_key = jax.random.fold_in(key, 21)
    subkeys = jax.random.split(base_key, 4)
    direction = direction_base(key)
    noise_part = jnp.clip(jax.random.normal(subkeys[0], (TOKENS, D), jnp.float32), -4.0, 4.0)
    row_scale = jnp.exp(jax.random.uniform(subkeys[1], (TOKENS, 1), jnp.float32, math.log(0.3), math.log(3.0)))
    column_ramp = 0.6 + 1.2 * jnp.arange(D, dtype=jnp.float32)[None, :] / D
    col_scale = jnp.exp(jax.random.uniform(subkeys[2], (1, D), jnp.float32, math.log(0.5), math.log(1.5))) * column_ramp
    along_coef = jax.random.uniform(subkeys[3], (TOKENS, 1), jnp.float32, -1.0, 1.0)
    values = noise_part * row_scale * col_scale + 3.0 * along_coef * direction[None, :]
    return values.astype(jnp.bfloat16)


def place_ends(values, key, smallest, largest):
    spot = [jax.random.randint(jax.random.fold_in(key, axis), (), 0, length) for axis, length in enumerate(values.shape)]
    main_axis = values.shape.index(max(values.shape))
    next_to = spot[:main_axis] + [(spot[main_axis] + 1) % values.shape[main_axis]] + spot[main_axis + 1:]
    return values.at[tuple(spot)].set(smallest).at[tuple(next_to)].set(largest)


def block_levels(stream_key, dims, cuts, low, top_value):
    def one(dim, blocks):
        draws = jax.random.uniform(jax.random.fold_in(jax.random.fold_in(stream_key, 6), dim), (blocks,), jnp.float32, low / len(cuts), top_value / len(cuts))
        return jnp.repeat(jnp.exp(draws), dims[dim] // blocks).reshape((-1,) + (1,) * (len(dims) - dim - 1))

    loudness = one(*cuts[0])
    for cut in cuts[1:]:
        loudness = loudness * one(*cut)
    return loudness


def assign_block(stream_key, own, number, rows, amount, top, limit, slope):
    sequence = jax.random.permutation(stream_key, amount)
    crowded, ordinary = load_shares(amount, rows * top, limit, slope, True), load_shares(amount, rows * top, limit, slope, False)
    places = jnp.arange(amount)

    def named(tallies, rotation):
        used = int((tallies > 0).sum())
        fixed = max(1, used // 4)
        moved = fixed + (places - fixed + rotation * (used - fixed)) % max(1, amount - fixed)
        return jnp.zeros((amount,), jnp.int32).at[sequence[jnp.where(places < fixed, places, moved)]].set(jnp.asarray(tallies, jnp.int32))

    tallies = jnp.where(number % 4 == 0, named(crowded, number // 4), named(ordinary, number - number // 4 - 1))
    mixed = jax.random.permutation(jax.random.fold_in(own, 3), amount)
    source_of, taker = mixed[0:amount // 2 * 2:2], mixed[1:amount // 2 * 2:2]
    margin = jnp.minimum(tallies[source_of] - 1, limit - tallies[taker]) // 2
    margin = jnp.where((source_of == sequence[0]) | (taker == sequence[0]) | (tallies[taker] == 0), 0, jnp.maximum(margin, 0))
    moved = jax.random.randint(jax.random.fold_in(own, 4), (amount // 2,), 0, 1 << 20) % (margin + 1)
    tallies = tallies.at[source_of].add(-moved).at[taker].add(moved)
    items = jnp.searchsorted(jnp.cumsum(tallies), jnp.arange(rows * top), side="right").astype(jnp.int32)
    grid = items.reshape(top, rows).T
    grid = grid[jax.random.permutation(jax.random.fold_in(own, 1), rows)]
    rotation = jax.random.randint(jax.random.fold_in(own, 2), (rows, 1), 0, top)
    return jnp.take_along_axis(grid, (jnp.arange(top)[None, :] + rotation) % top, axis=1)


def load_shares(number_of, total, most, lean, full):
    weights = [(1 << 20) // math.isqrt(grade ** lean) + 1 for grade in range(1, number_of + 1)]
    largest = most if full else min(most, max(-(-total // number_of), total * weights[0] // sum(weights)))
    least = 1 if total - largest >= number_of - 1 else 0
    holding, surplus = [largest] + [least] * (number_of - 1), total - largest - least * (number_of - 1)
    while surplus > 0:
        free = [i for i in range(1, number_of) if holding[i] < largest] or [i for i in range(1, number_of) if holding[i] < most]
        mass, remaining = sum([weights[i] for i in free]), surplus
        for i in free:
            more = min(most - holding[i], max(1, remaining * weights[i] // mass), surplus)
            holding[i] = holding[i] + more
            surplus = surplus - more
    return np.array(holding)


def noise(key, extent, spread, bound, cuts=(), kind=jnp.bfloat16):
    factor_of = block_levels(key, extent, cuts, -0.22, 0.18) if cuts else 1.0
    drawn = jax.random.normal(key, extent, jnp.float32) * spread * factor_of
    return jnp.minimum(jnp.maximum(drawn, -bound), bound).astype(kind)


def setup_inputs(seed: int = 0) -> dict:
    seeds = jax.random.split(jax.random.key(seed), 10)
    attn_part = noise(seeds[0], (HG, TOKENS, D), 0.4, 2.5, ((0, 4), (1, 8)))
    resid = draw_resid(jax.random.fold_in(seeds[9], 71), 0)
    refusal = draw_refusal(jax.random.fold_in(seeds[9], 71), 0)
    norm_gain = jnp.clip(0.5 + 1.0 * jax.random.uniform(seeds[3], (D,), jnp.float32) ** block_levels(seeds[3], (D,), ((0, 4),), -0.2, 0.2), 0.5, 1.5)
    route_ids_keys = jax.random.split(jax.random.fold_in(seeds[4], 1), TOKENS // TOK_GRP)
    route_ids_turns = jax.random.permutation(jax.random.fold_in(seeds[4], 3), TOKENS // TOK_GRP)
    route_ids = jax.vmap(lambda own, number: assign_block(jax.random.fold_in(seeds[4], 2), own, number, TOK_GRP, EXPERTS, TOP, CAP, 2))(route_ids_keys, route_ids_turns).reshape((TOKENS, TOP))
    gate_q = place_ends(jax.random.randint(seeds[5], (TOKENS, TOP), 16, 256), jax.random.fold_in(seeds[5], 1), 16, 255).astype(jnp.int32)
    w_gate = noise(seeds[6], (EXPERTS, D, H), D ** -0.5, 0.0625, ((0, 8), (2, 4)))
    w_up = noise(seeds[7], (EXPERTS, D, H), D ** -0.5, 0.0625, ((0, 8), (2, 4)))
    w_down = noise(seeds[8], (EXPERTS, H, D), H ** -0.5, 0.125, ((0, 8), (1, 4)))
    return {"attn_part": attn_part, "resid": resid, "refusal": refusal, "norm_gain": norm_gain, "route_ids": route_ids, "gate_q": gate_q, "w_gate": w_gate, "w_up": w_up, "w_down": w_down}


EPSILON = 1e-06
GATE_UNIT = 128.0

def route_tables(route_ids, gate_q, experts, slot_count):
    row_count = route_ids.shape[0]
    matches = route_ids[:, :, None] == jnp.arange(experts, dtype=jnp.int32)[None, None, :]
    named_count = lax.optimization_barrier(jnp.sum(matches.astype(jnp.int32), axis=1, dtype=jnp.int32))
    weight = lax.optimization_barrier(jnp.sum(jnp.where(matches, gate_q[:, :, None], 0), axis=1, dtype=jnp.int32))
    before = jnp.cumsum(named_count, axis=0, dtype=jnp.int32) - named_count
    placed = (named_count[:, :, None] == 1) & (before[:, :, None] == jnp.arange(slot_count, dtype=jnp.int32)[None, None, :])
    select = placed.reshape(row_count, experts * slot_count)
    scaled = jnp.where(placed, weight[:, :, None].astype(jnp.float32) / GATE_UNIT, 0.0)
    scaled = scaled.reshape(row_count, experts * slot_count)
    return (select.astype(jnp.bfloat16).T, scaled.astype(jnp.bfloat16))

def reference(attn_part, resid, refusal, norm_gain, route_ids, gate_q, w_gate, w_up, w_down):
    highest = lax.Precision.HIGHEST
    summed_heads = resid.astype(jnp.float32) + lax.optimization_barrier(jnp.sum(attn_part.astype(jnp.float32), axis=0))
    unit = refusal * lax.rsqrt(jnp.sum(refusal * refusal) + EPSILON)
    along = jnp.dot(summed_heads, unit, precision=highest)
    projected = summed_heads - along[:, None] * unit[None, :]
    mean_square = lax.optimization_barrier(jnp.mean(projected * projected, axis=1, keepdims=True))
    normed = (projected * lax.rsqrt(mean_square + EPSILON) * norm_gain[None, :]).astype(jnp.bfloat16)
    group_rows = normed.reshape(N_EXP, TOK_GRP, D).astype(jnp.float32)

    def tables(ids_block, gates_block):
        return route_tables(ids_block, gates_block, EXPERTS, CAP)
    select, scaled = jax.vmap(tables)(route_ids.reshape(N_EXP, TOK_GRP, TOP), gate_q.reshape(N_EXP, TOK_GRP, TOP))
    select_by_expert = select.reshape(N_EXP, EXPERTS, CAP, TOK_GRP).transpose(1, 0, 2, 3)
    scaled_by_expert = scaled.reshape(N_EXP, TOK_GRP, EXPERTS, CAP).transpose(2, 0, 1, 3)
    slice_width = H // N_TP

    def one_expert(carry, items):
        picks, weights, gate_weight, up_weight, down_weight = items
        chosen = jnp.einsum('gct,gtd->gcd', picks.astype(jnp.float32), group_rows, precision=highest)
        chosen = chosen.astype(jnp.bfloat16).reshape(N_EXP * CAP, D)
        gate_act = jnp.dot(chosen, gate_weight, preferred_element_type=jnp.float32)
        up_act = jnp.dot(chosen, up_weight, preferred_element_type=jnp.float32)
        activation = (jax.nn.silu(gate_act) * up_act).astype(jnp.bfloat16)
        total = jnp.zeros((N_EXP * CAP, D), jnp.float32)
        for group_index in range(N_TP):
            low = group_index * slice_width
            term = jnp.dot(activation[:, low:low + slice_width], down_weight[low:low + slice_width, :], preferred_element_type=jnp.float32)
            total = total + lax.optimization_barrier(term.astype(jnp.bfloat16)).astype(jnp.float32)
        added = jnp.einsum('gtc,gcd->gtd', weights.astype(jnp.float32), total.reshape(N_EXP, CAP, D), precision=highest)
        return (carry + added, None)
    start = jnp.zeros((N_EXP, TOK_GRP, D), jnp.float32)
    mixed, _ = lax.scan(one_expert, start, (select_by_expert, scaled_by_expert, w_gate, w_up, w_down))
    return (projected + mixed.reshape(TOKENS, D)).astype(jnp.bfloat16)
```

```python
import functools
import jax
import jax.numpy as jnp
from jax import lax
from jax.experimental import pallas as pl
from jax.experimental.pallas import tpu as pltpu
from jax.sharding import PartitionSpec as P

EPSILON = 1e-06
GATE_UNIT = 128.0
LANES = 128
VMEM_LIMIT = 56 << 20
F32 = jnp.float32
BF16 = jnp.bfloat16


def vmem():
    return pl.BlockSpec(memory_space=pltpu.VMEM)


def smem():
    return pl.BlockSpec(memory_space=pltpu.SMEM)


def params():
    return pltpu.CompilerParams(vmem_limit_bytes=VMEM_LIMIT)


def swap(value, axis, bit):
    count = lax.axis_size(axis)
    return lax.ppermute(value, axis, [(i, i ^ bit) for i in range(count)])


def exp_bits(exp_count):
    plane = [1 << i for i in range(1, exp_count.bit_length() - 1)]
    x_bits, y_bits = plane[: len(plane) // 2], plane[len(plane) // 2 :]
    return [1] if exp_count > 1 else [], (x_bits + y_bits, y_bits + x_bits)


def relative_order(bits):
    order = [0]
    for bit in reversed(bits):
        order = order + [pattern ^ bit for pattern in order]
    return order


def three_parts(value):
    first = value.astype(BF16)
    rest = value - first.astype(F32)
    second = rest.astype(BF16)
    third = (rest - second.astype(F32)).astype(BF16)
    return first.astype(F32), second.astype(F32), third.astype(F32)


def sum_kernel(*refs):
    parts, (resid, unit, message, summed) = refs[:-4], refs[-4:]
    total = parts[0][...].astype(F32)
    for part in parts[1:]:
        total = total + part[...].astype(F32)
    rows = resid[...].astype(F32) + total
    summed[...] = rows
    u = unit[...]
    inner = jnp.sum(rows * u, axis=1, keepdims=True)
    own = inner / (jnp.sum(u * u) + EPSILON)
    width = rows.shape[1]
    message[:, :width] = (rows - own * u).astype(BF16)
    first, second, third = three_parts(inner)
    lane = lax.broadcasted_iota(jnp.int32, (rows.shape[0], LANES), 1)
    packed = jnp.where(lane == 0, first, jnp.where(lane == 1, second, jnp.where(lane == 2, third, 0.0)))
    message[:, width:] = packed.astype(BF16)


def norm_kernel(tp_count, me, unit, ids, gates, *refs):
    messages, gains = refs[:tp_count], refs[tp_count : 2 * tp_count]
    outs, along_out = refs[2 * tp_count : -1], refs[-1]
    width = gains[0].shape[1]
    rows = messages[0].shape[0]
    inner, units = [], []
    for k in range(tp_count):
        tail = messages[k][:, width:].astype(F32)
        inner.append(jnp.sum(tail, axis=1, keepdims=True))
        units.append(unit[:, pl.ds(pl.multiple_of((me[0] ^ k) * width, LANES), width)])
    along = functools.reduce(lambda a, b: a + b, inner)
    along_out[...] = jnp.broadcast_to(along, along_out.shape)
    projected, square = [], 0.0
    for k in range(tp_count):
        u = units[k]
        own = inner[k] / (jnp.sum(u * u) + EPSILON)
        value = messages[k][:, :width].astype(F32) + (own - along) * u
        square = square + jnp.sum(value * value, axis=1, keepdims=True)
        projected.append(value)
    inverse = lax.rsqrt(square / (width * tp_count) + EPSILON)
    half = rows // len(outs)
    for k in range(tp_count):
        normed = (projected[k] * inverse * gains[k][...]).astype(BF16)
        for i, out in enumerate(outs):
            out[:, k * width : (k + 1) * width] = normed[i * half : (i + 1) * half]
    lane = lax.broadcasted_iota(jnp.int32, (rows, LANES), 1)
    table = jnp.zeros((rows, LANES), F32)
    for i in range(ids.shape[1]):
        table = table + jnp.where(ids[:, i : i + 1] == lane, gates[:, i : i + 1].astype(F32), 0.0)
    table = (table / GATE_UNIT).astype(BF16)
    for i, out in enumerate(outs):
        out[:, tp_count * width :] = table[i * half : (i + 1) * half]


def up_kernel(piece_count, me, first, w_gate, w_up, *refs):
    pieces, (out, rows, table, gate_acc, up_acc) = refs[:piece_count], refs[piece_count:]
    expert, k = pl.program_id(0), pl.program_id(1)
    depth = w_gate.shape[1]
    full = rows.shape[1]

    @pl.when((expert == 0) & (k == 0))
    def _():
        height = pieces[0].shape[0]
        for i, piece in enumerate(pieces):
            rows[i * height : (i + 1) * height, :] = piece[:, :full]
            table[i * height : (i + 1) * height, :] = piece[:, full:]

    x = rows[:, pl.ds(pl.multiple_of(k * depth, LANES), depth)]
    gate = jnp.dot(x, w_gate[0], preferred_element_type=F32)
    up = jnp.dot(x, w_up[0], preferred_element_type=F32)

    @pl.when(k == 0)
    def _():
        gate_acc[...] = gate
        up_acc[...] = up

    @pl.when(k > 0)
    def _():
        gate_acc[...] += gate
        up_acc[...] += up

    @pl.when(k == pl.num_programs(1) - 1)
    def _():
        lane = lax.broadcasted_iota(jnp.int32, table.shape, 1)
        weight = jnp.sum(jnp.where(lane == first[0] + expert, table[...].astype(F32), 0.0), axis=1, keepdims=True)
        out[...] = (jax.nn.silu(gate_acc[...]) * up_acc[...] * weight).astype(BF16)


def down_kernel(me, activation, w_down, keep, send):
    weights = w_down[...].reshape(-1, w_down.shape[2])
    total = jnp.dot(activation[...], weights, preferred_element_type=F32).astype(BF16)
    half = keep.shape[0]
    keep[...] = total[:half]
    send[...] = total[half:]


def gather_rows(halves, core, orders):
    gathered = []
    for half, order in zip(halves, orders):
        pieces = {0: half}
        for bit in list(order) + core:
            pieces.update({pattern ^ bit: swap(piece, "exp", bit) for pattern, piece in list(pieces.items())})
        gathered.append(pieces)
    return gathered


def add(a, b):
    return (a.astype(F32) + b.astype(F32)).astype(BF16)


def scatter_rows(keep, send, core, orders):
    got = swap(send, "exp", core[0])
    results = []
    height = keep.shape[0] // len(orders)
    for i, order in enumerate(orders):
        mine, theirs = keep[i * height : (i + 1) * height], got[i * height : (i + 1) * height]
        for bit in order:
            middle = mine.shape[0] // 2
            away = add(mine[middle:], theirs[middle:])
            mine = add(mine[:middle], theirs[:middle])
            theirs = swap(away, "exp", bit)
        results.append((mine, theirs))
    return results


def local(attn_part, resid, refusal, norm_gain, route_ids, gate_q, w_gate, w_up, w_down):
    tp_count = lax.axis_size("tp")
    exp_count = lax.axis_size("exp")
    rows, cols = resid.shape
    full = refusal.shape[0]
    local_experts, _, hidden = w_gate.shape
    t = lax.axis_index("tp")
    me = t.astype(jnp.int32).reshape(1)
    first = (lax.axis_index("exp") * local_experts).astype(jnp.int32).reshape(1)
    core, orders = exp_bits(exp_count)
    half = rows // 2

    own = [lax.dynamic_slice_in_dim(attn_part[0], (t ^ k) * cols, cols, 1) for k in range(tp_count)]
    heads = [own[0]] + [swap(own[k], "tp", k) for k in range(1, tp_count)]
    gain = norm_gain.reshape(1, cols)
    gains = [gain] + [swap(gain, "tp", k) for k in range(1, tp_count)]
    unit = (refusal * lax.rsqrt(jnp.sum(refusal * refusal) + EPSILON)).reshape(1, full)
    unit_cols = lax.dynamic_slice_in_dim(unit, t * cols, cols, 1)

    message, summed = pl.pallas_call(
        sum_kernel,
        out_shape=(
            jax.ShapeDtypeStruct((rows, cols + LANES), BF16),
            jax.ShapeDtypeStruct((rows, cols), F32),
        ),
        in_specs=[vmem()] * (tp_count + 2),
        out_specs=(vmem(), vmem()),
        compiler_params=params(),
        name="sum_heads",
    )(*heads, resid, unit_cols)
    messages = [message] + [swap(message, "tp", k) for k in range(1, tp_count)]

    *halves, along = pl.pallas_call(
        functools.partial(norm_kernel, tp_count),
        out_shape=(
            jax.ShapeDtypeStruct((half, full + LANES), BF16),
            jax.ShapeDtypeStruct((half, full + LANES), BF16),
            jax.ShapeDtypeStruct((rows, LANES), F32),
        ),
        in_specs=[smem()] + [vmem()] * (3 + 2 * tp_count),
        out_specs=(vmem(), vmem(), vmem()),
        compiler_params=params(),
        name="norm_rows",
    )(me, unit, route_ids, gate_q, *messages, *gains)

    gathered = gather_rows(halves, core, orders)
    pieces = []
    for bit in [0] + core:
        for found, order in zip(gathered, orders):
            pieces += [found[bit ^ pattern] for pattern in relative_order(order)]
    total_rows = rows * exp_count

    activation = pl.pallas_call(
        functools.partial(up_kernel, len(pieces)),
        out_shape=jax.ShapeDtypeStruct((total_rows, local_experts * hidden), BF16),
        grid_spec=pltpu.PrefetchScalarGridSpec(
            num_scalar_prefetch=2,
            grid=(local_experts, tp_count),
            in_specs=[
                pl.BlockSpec((1, cols, hidden), lambda e, k, me, first: (e, me[0] ^ k, 0)),
                pl.BlockSpec((1, cols, hidden), lambda e, k, me, first: (e, me[0] ^ k, 0)),
            ]
            + [vmem()] * len(pieces),
            out_specs=pl.BlockSpec((total_rows, hidden), lambda e, k, me, first: (0, e)),
            scratch_shapes=[
                pltpu.VMEM((total_rows, full), BF16),
                pltpu.VMEM((total_rows, LANES), BF16),
                pltpu.VMEM((total_rows, hidden), F32),
                pltpu.VMEM((total_rows, hidden), F32),
            ],
        ),
        compiler_params=params(),
        name="gate_up",
    )(me, first, w_gate, w_up, *pieces)

    chunks = 2 if cols % (2 * LANES) == 0 else 1
    width = cols // chunks
    outs = []
    for chunk in range(chunks):
        keep, send = pl.pallas_call(
            down_kernel,
            out_shape=[jax.ShapeDtypeStruct((total_rows // 2, tp_count * width), BF16)] * 2,
            grid_spec=pltpu.PrefetchScalarGridSpec(
                num_scalar_prefetch=1,
                grid=(tp_count,),
                in_specs=[
                    vmem(),
                    pl.BlockSpec(
                        (local_experts, hidden, width),
                        lambda k, me, chunk=chunk: (0, 0, (me[0] ^ k) * chunks + chunk),
                    ),
                ],
                out_specs=[pl.BlockSpec((total_rows // 2, width), lambda k, me: (0, k))] * 2,
            ),
            compiler_params=params(),
            name="down",
        )(me, activation, w_down)
        results = scatter_rows(keep, send, core, orders)
        columns = []
        for k in range(tp_count):
            part = [
                add(mine[:, k * width : (k + 1) * width], theirs[:, k * width : (k + 1) * width])
                for mine, theirs in results
            ]
            part = jnp.concatenate(part, axis=0)
            columns.append(part if k == 0 else swap(part, "tp", k))
        mixed = functools.reduce(lambda a, b: a + b, [c.astype(F32) for c in columns])
        here = slice(chunk * width, (chunk + 1) * width)
        projected = summed[:, here] - along[:, :1] * unit_cols[:, here]
        outs.append((projected + mixed).astype(BF16))
    return jnp.concatenate(outs, axis=1)


def solution(mesh):
    return jax.shard_map(
        local,
        mesh=mesh,
        in_specs=(
            P("tp", "exp", None),
            P("exp", "tp"),
            P(),
            P("tp"),
            P("exp", None),
            P("exp", None),
            P("exp", None, "tp"),
            P("exp", None, "tp"),
            P("exp", "tp", None),
        ),
        out_specs=P("exp", "tp"),
        check_vma=False,
    )
```

```python
import functools
import jax
import jax.numpy as jnp
from jax import lax
from jax.experimental import pallas as pl
from jax.experimental.pallas import tpu as pltpu
from jax.sharding import PartitionSpec as P

EPSILON = 1e-06
GATE_UNIT = 128.0
LANES = 128
PARTS = 3
F32 = jnp.float32
BF16 = jnp.bfloat16


def vmem():
    return pl.BlockSpec(memory_space=pltpu.VMEM)


def smem():
    return pl.BlockSpec(memory_space=pltpu.SMEM)


def params(mib):
    return pltpu.CompilerParams(vmem_limit_bytes=mib << 20)


def shape(*dims, dtype=BF16):
    return jax.ShapeDtypeStruct(dims, dtype)


def swap(value, axis, bit):
    count = lax.axis_size(axis)
    return lax.ppermute(value, axis, [(i, i ^ bit) for i in range(count)])


def exp_bits(exp_count):
    plane = [1 << i for i in range(1, exp_count.bit_length() - 1)]
    x_bits, y_bits = plane[: len(plane) // 2], plane[len(plane) // 2 :]
    return 1, (x_bits + y_bits, y_bits + x_bits)


def relative_order(bits):
    order = [0]
    for bit in reversed(bits):
        order = order + [pattern ^ bit for pattern in order]
    return order


def three_parts(value):
    first = value.astype(BF16).astype(F32)
    second = (value - first).astype(BF16).astype(F32)
    return first, second, (value - first - second).astype(BF16).astype(F32)


def unit_of(refusal):
    return refusal * lax.rsqrt(jnp.sum(refusal * refusal) + EPSILON)


def cut_kernel(me, attn, resid, refusal, *outs):
    slices, inner = outs[:-1], outs[-1]
    width = resid.shape[1]
    for k, out in enumerate(slices):
        out[...] = attn[:, pl.ds(pl.multiple_of((me[0] ^ k) * width, LANES), width)]
    u = unit_of(refusal[...])
    scale = lax.rsqrt(jnp.sum(refusal[...] * refusal[...]) + EPSILON)
    own = refusal[:, pl.ds(pl.multiple_of(me[0] * width, LANES), width)] * scale
    total = jnp.sum(attn[...].astype(F32) * u, axis=1, keepdims=True)
    total = total + jnp.sum(resid[...].astype(F32) * own, axis=1, keepdims=True)
    inner[...] = jnp.broadcast_to(total, inner.shape)


def project_kernel(tp_count, experts, me, resid, refusal, gain, ids, gates, *refs):
    parts, inner, (message, projected) = refs[:tp_count], refs[tp_count : 2 * tp_count], refs[2 * tp_count :]
    rows, width = resid.shape
    total = parts[0][...].astype(F32)
    for part in parts[1:]:
        total = total + part[...].astype(F32)
    along = inner[0][...]
    for share in inner[1:]:
        along = along + share[...]
    scale = lax.rsqrt(jnp.sum(refusal[...] * refusal[...]) + EPSILON)
    u = refusal[:, pl.ds(pl.multiple_of(me[0] * width, LANES), width)] * scale
    value = resid[...].astype(F32) + total - along[:, :1] * u
    projected[...] = value
    message[:, :width] = (value * gain[...]).astype(BF16)
    lane = lax.broadcasted_iota(jnp.int32, (rows, message.shape[1] - width), 1)
    tail = jnp.zeros(lane.shape, F32)
    for i in range(ids.shape[1]):
        tail = tail + jnp.where(ids[:, i : i + 1] == lane, gates[:, i : i + 1].astype(F32), 0.0)
    tail = tail / GATE_UNIT
    for i, part in enumerate(three_parts(jnp.sum(value * value, axis=1, keepdims=True))):
        tail = jnp.where(lane == experts + i, part, tail)
    message[:, width:] = tail.astype(BF16)


def up_kernel(spots, start, last, full, experts, me, first, w_gate, w_up, *refs):
    count = len(spots)
    pieces, refs = refs[:count], refs[count:]
    if not start:
        refs = refs[3:] if not last else refs
    if last:
        gate_in, up_in, side_in, out, x, side = refs
    else:
        gate_acc, up_acc, side, x = refs
    expert = pl.program_id(0)
    depth = w_gate.shape[1]

    @pl.when(expert == 0)
    def _():
        for piece, spot in zip(pieces, spots):
            height = piece.shape[0] // len(spot)
            for i, place in enumerate(spot):
                here, there = slice(i * height, (i + 1) * height), slice(place * height, (place + 1) * height)
                x[there, :] = piece[here, :depth]
                tail = piece[here, depth:].astype(F32)
                lane = lax.broadcasted_iota(jnp.int32, tail.shape, 1)
                if not start:
                    before = side_in if last else side
                    tail = before[there, :] + jnp.where(lane >= experts, tail, 0.0)
                side[there, :] = tail

    gate = jnp.dot(x[...], w_gate[0], preferred_element_type=F32)
    up = jnp.dot(x[...], w_up[0], preferred_element_type=F32)
    if start:
        gate_acc[expert] = gate
        up_acc[expert] = up
    elif not last:
        gate_acc[expert] += gate
        up_acc[expert] += up
    else:
        beside = side[...]
        lane = lax.broadcasted_iota(jnp.int32, beside.shape, 1)
        weight = jnp.sum(jnp.where(lane == first[0] + expert, beside, 0.0), axis=1, keepdims=True)
        square = jnp.sum(jnp.where(lane >= experts, beside, 0.0), axis=1, keepdims=True)
        inverse = lax.rsqrt(square / full + EPSILON)
        gate = (gate_in[expert] + gate) * inverse
        up = (up_in[expert] + up) * inverse
        out[...] = (jax.nn.silu(gate) * up * weight).astype(BF16)


def down_kernel(order, me, activation, w_down, keep, send):
    weights = w_down[...].reshape(-1, w_down.shape[2])
    total = jnp.dot(activation[...], weights, preferred_element_type=F32).astype(BF16)
    height = total.shape[0] // len(order)
    middle = len(order) // 2
    for i, pattern in enumerate(order):
        out = keep if i < middle else send
        place = i % middle
        out[place * height : (place + 1) * height, :] = total[pattern * height : (pattern + 1) * height]


def gather_rows(block, order, core, merge):
    found = [([0], block)]
    for bit in list(order) + [core]:
        found += [([pattern ^ bit for pattern in patterns], swap(piece, "exp", bit)) for patterns, piece in found]
        if merge:
            found = [(sum((p for p, _ in found), []), jnp.concatenate([piece for _, piece in found], axis=0))]
    return found


def add(a, b):
    return (a.astype(F32) + b.astype(F32)).astype(BF16)


def local(attn_part, resid, refusal, norm_gain, route_ids, gate_q, w_gate, w_up, w_down):
    tp_count = lax.axis_size("tp")
    exp_count = lax.axis_size("exp")
    rows, cols = resid.shape
    full = refusal.shape[0]
    local_experts, _, hidden = w_gate.shape
    experts = local_experts * exp_count
    tail = -(-(experts + PARTS) // LANES) * LANES
    total_rows = rows * exp_count
    me = lax.axis_index("tp").astype(jnp.int32).reshape(1)
    first = (lax.axis_index("exp") * local_experts).astype(jnp.int32).reshape(1)
    core, orders = exp_bits(exp_count)
    refusal = refusal.reshape(1, full)

    *slices, inner = pl.pallas_call(
        cut_kernel,
        out_shape=[shape(rows, cols)] * tp_count + [shape(rows, LANES, dtype=F32)],
        in_specs=[smem()] + [vmem()] * 3,
        out_specs=[vmem()] * (tp_count + 1),
        compiler_params=params(8),
        name="cut_heads",
    )(me, attn_part[0], resid, refusal)
    heads = slices[:1] + [swap(slices[k], "tp", k) for k in range(1, tp_count)]
    shares = [inner] + [swap(inner, "tp", k) for k in range(1, tp_count)]

    message, projected = pl.pallas_call(
        functools.partial(project_kernel, tp_count, experts),
        out_shape=[shape(rows, cols + tail), shape(rows, cols, dtype=F32)],
        in_specs=[smem()] + [vmem()] * (5 + 2 * tp_count),
        out_specs=[vmem()] * 2,
        compiler_params=params(8),
        name="project",
    )(me, resid, refusal, norm_gain.reshape(1, cols), route_ids, gate_q, *heads, *shares)
    messages = [message] + [swap(message, "tp", k) for k in range(1, tp_count)]

    state = []
    for k in range(tp_count):
        found = gather_rows(messages[k], orders[k % 2], core, exp_count > 8)
        spots, pieces = [s for s, _ in found], [p for _, p in found]
        start, last = k == 0, k == tp_count - 1
        acc = pltpu.VMEM((local_experts, total_rows, hidden), F32)
        if last:
            out_shape = [shape(total_rows, local_experts * hidden)]
            out_specs = [pl.BlockSpec((total_rows, hidden), lambda e, *_: (0, e))]
        else:
            out_shape = [acc, acc, pltpu.VMEM((total_rows, tail), F32)]
            out_specs = [vmem()] * 3
        weights = pl.BlockSpec((1, cols, hidden), lambda e, me, first, k=k: (e, me[0] ^ k, 0))
        state = pl.pallas_call(
            functools.partial(up_kernel, spots, start, last, full, experts),
            out_shape=out_shape,
            grid_spec=pltpu.PrefetchScalarGridSpec(
                num_scalar_prefetch=2,
                grid=(local_experts,),
                in_specs=[weights, weights] + [vmem()] * (len(pieces) + len(state)),
                out_specs=out_specs,
                scratch_shapes=[pltpu.VMEM((total_rows, cols), BF16)] + ([pltpu.VMEM((total_rows, tail), F32)] if last else []),
            ),
            input_output_aliases={} if start or last else {4 + len(pieces) + i: i for i in range(3)},
            compiler_params=params(24),
            cost_estimate=pl.CostEstimate(
                flops=4 * total_rows * cols * hidden * local_experts,
                bytes_accessed=4 * cols * hidden * local_experts,
                transcendentals=0,
            ),
            name="gate_up",
        )(me, first, w_gate, w_up, *pieces, *state)
    activation = state[0]

    steps = 2 if cols % (2 * LANES) == 0 else 1
    width = cols // steps
    mixed = projected
    columns = []
    for k in reversed(range(tp_count)):
        order = orders[k % 2]
        keep, send = pl.pallas_call(
            functools.partial(down_kernel, relative_order([core] + order)),
            out_shape=[shape(total_rows // 2, cols)] * 2,
            grid_spec=pltpu.PrefetchScalarGridSpec(
                num_scalar_prefetch=1,
                grid=(steps,),
                in_specs=[
                    vmem(),
                    pl.BlockSpec((local_experts, hidden, width), lambda i, me, k=k: (0, 0, (me[0] ^ k) * steps + i)),
                ],
                out_specs=[pl.BlockSpec((total_rows // 2, width), lambda i, me: (0, i))] * 2,
            ),
            compiler_params=params(24),
            cost_estimate=pl.CostEstimate(
                flops=2 * total_rows * cols * hidden * local_experts,
                bytes_accessed=2 * cols * hidden * local_experts,
                transcendentals=0,
            ),
            name="down",
        )(me, activation, w_down)
        mine, theirs = keep, swap(send, "exp", core)
        for bit in order:
            middle = mine.shape[0] // 2
            away = add(mine[middle:], theirs[middle:])
            mine, theirs = add(mine[:middle], theirs[:middle]), swap(away, "exp", bit)
        if k:
            columns.append(swap(add(mine, theirs), "tp", k))
        else:
            columns += [mine, theirs]
    for column in columns:
        mixed = mixed + column.astype(F32)
    return mixed.astype(BF16)


def solution(mesh):
    return jax.shard_map(
        local,
        mesh=mesh,
        in_specs=(
            P("tp", "exp", None),
            P("exp", "tp"),
            P(),
            P("tp"),
            P("exp", None),
            P("exp", None),
            P("exp", None, "tp"),
            P("exp", None, "tp"),
            P("exp", "tp", None),
        ),
        out_specs=P("exp", "tp"),
        check_vma=False,
    )
```

```python
import functools
import jax
import jax.numpy as jnp
from jax import lax
from jax.experimental import pallas as pl
from jax.experimental.pallas import tpu as pltpu
from jax.sharding import PartitionSpec as P

EPSILON = 1e-06
GATE_UNIT = 128.0
LANES = 128
PARTS = 3
F32 = jnp.float32
BF16 = jnp.bfloat16


def vmem():
    return pl.BlockSpec(memory_space=pltpu.VMEM)


def smem():
    return pl.BlockSpec(memory_space=pltpu.SMEM)


def on_chip(value):
    return pltpu.with_memory_space_constraint(value, pltpu.VMEM)


def off_chip(value):
    return pltpu.with_memory_space_constraint(value, pltpu.HBM)


def params(mib):
    return pltpu.CompilerParams(vmem_limit_bytes=mib << 20)


def shape(*dims, dtype=BF16):
    return jax.ShapeDtypeStruct(dims, dtype)


def swap(value, axis, bit):
    count = lax.axis_size(axis)
    return lax.ppermute(value, axis, [(i, i ^ bit) for i in range(count)])


def exp_bits(exp_count):
    plane = [1 << i for i in range(1, exp_count.bit_length() - 1)]
    x_bits, y_bits = plane[: len(plane) // 2], plane[len(plane) // 2 :]
    return 1, (x_bits + y_bits, y_bits + x_bits)


def relative_order(bits):
    order = [0]
    for bit in reversed(bits):
        order = order + [pattern ^ bit for pattern in order]
    return order


def three_parts(value):
    first = value.astype(BF16).astype(F32)
    second = (value - first).astype(BF16).astype(F32)
    return first, second, (value - first - second).astype(BF16).astype(F32)


def cut_kernel(me, attn_hbm, resid_hbm, refusal_hbm, *refs):
    slices, (base, share, unit, attn, resid, refusal, sems) = refs[:-7], refs[-7:]
    copies = [
        pltpu.make_async_copy(source, target, sems.at[i])
        for i, (source, target) in enumerate(((attn_hbm, attn), (resid_hbm, resid), (refusal_hbm, refusal)))
    ]
    for copy in copies:
        copy.start()
    for copy in copies:
        copy.wait()
    rows, width = resid.shape
    scale = lax.rsqrt(jnp.sum(refusal[...] * refusal[...]) + EPSILON)
    own = refusal[:, pl.ds(pl.multiple_of(me[0] * width, LANES), width)] * scale
    unit[...] = own
    total = jnp.sum(attn[...].astype(F32) * (refusal[...] * scale), axis=1, keepdims=True)
    total = total + jnp.sum(resid[...].astype(F32) * own, axis=1, keepdims=True)
    share[...] = jnp.broadcast_to(total, share.shape)
    lane = lax.broadcasted_iota(jnp.int32, share.shape, 1)
    tail = jnp.zeros(share.shape, F32)
    for i, part in enumerate(three_parts(total)):
        tail = jnp.where(lane == i, part, tail)
    tail = tail.astype(BF16)
    for i, out in enumerate(slices):
        out[:, :width] = attn[:, pl.ds(pl.multiple_of((me[0] ^ (i + 1)) * width, LANES), width)]
        out[:, width:] = tail
    here = attn[:, pl.ds(pl.multiple_of(me[0] * width, LANES), width)]
    base[...] = resid[...].astype(F32) + here.astype(F32)


def project_kernel(experts, base, share, unit, gain, ids, gates, *refs):
    parts, (message, projected) = refs[:-2], refs[-2:]
    rows, width = base.shape
    total, along = base[...], share[:, :1]
    for part in parts:
        total = total + part[:, :width].astype(F32)
        along = along + jnp.sum(part[:, width:].astype(F32), axis=1, keepdims=True)
    value = total - along * unit[...]
    projected[...] = value
    message[:, :width] = (value * gain[...]).astype(BF16)
    lane = lax.broadcasted_iota(jnp.int32, (rows, message.shape[1] - width), 1)
    tail = jnp.zeros(lane.shape, F32)
    for i in range(ids.shape[1]):
        tail = tail + jnp.where(ids[:, i : i + 1] == lane, gates[:, i : i + 1].astype(F32), 0.0)
    tail = tail / GATE_UNIT
    for i, part in enumerate(three_parts(jnp.sum(value * value, axis=1, keepdims=True))):
        tail = jnp.where(lane == experts + i, part, tail)
    message[:, width:] = tail.astype(BF16)


def up_kernel(start, last, chunks, ahead, full, experts, me, first, w_gate, w_up, down_hbm, *refs):
    *refs, sem = refs
    x = refs[-1 - last]
    held_down = refs[-2 - last]
    if last:
        out, side = refs[-4], refs[-1]
        pieces, (gate_in, up_in, side_in) = refs[:-7], refs[-7:-4]
    else:
        gate_acc, up_acc, side = refs[-5:-2]
        pieces = refs[:-5] if start else refs[:-8]
    expert = pl.program_id(0)
    columns = held_down.shape[2]
    block = (me[0] ^ ahead) // (columns // (x.shape[1] // chunks))
    copy = pltpu.make_async_copy(
        down_hbm.at[:, :, pl.ds(pl.multiple_of(block * columns, LANES), columns)], held_down, sem
    )
    width = x.shape[1] // chunks

    @pl.when(expert == 0)
    def _():
        copy.start()
        height = pieces[0].shape[0] // chunks
        for i, piece in enumerate(pieces):
            there = slice(i * height, (i + 1) * height)
            for j in range(chunks):
                here = slice(j * height, (j + 1) * height)
                slot = (me[0] & (chunks - 1)) ^ j
                x[there, pl.ds(pl.multiple_of(slot * width, LANES), width)] = piece[here, :width]
                tail = piece[here, width:].astype(F32)
                lane = lax.broadcasted_iota(jnp.int32, tail.shape, 1)
                if j or not start:
                    before = side_in if last and not j else side
                    tail = before[there, :] + jnp.where(lane >= experts, tail, 0.0)
                side[there, :] = tail

    gate = jnp.dot(x[...], w_gate[0], preferred_element_type=F32)
    up = jnp.dot(x[...], w_up[0], preferred_element_type=F32)
    if start:
        gate_acc[expert] = gate
        up_acc[expert] = up
    elif not last:
        gate_acc[expert] += gate
        up_acc[expert] += up
    else:
        beside = side[...]
        lane = lax.broadcasted_iota(jnp.int32, beside.shape, 1)
        weight = jnp.sum(jnp.where(lane == first[0] + expert, beside, 0.0), axis=1, keepdims=True)
        square = jnp.sum(jnp.where(lane >= experts, beside, 0.0), axis=1, keepdims=True)
        inverse = lax.rsqrt(square / full + EPSILON)
        gate = (gate_in[expert] + gate) * inverse
        up = (up_in[expert] + up) * inverse
        out[...] = (jax.nn.silu(gate) * up * weight).astype(BF16)

    @pl.when(expert == pl.num_programs(0) - 1)
    def _():
        copy.wait()


def down_kernel(order, place, cols, me, activation, w_down, keep, send):
    width = keep.shape[1]
    slot = (me[0] ^ place) & (w_down.shape[2] // cols - 1)
    here = pl.ds(pl.multiple_of(slot * cols + pl.program_id(0) * width, LANES), width)
    weights = w_down[:, :, here].reshape(-1, width)
    total = jnp.dot(activation[...], weights, preferred_element_type=F32).astype(BF16)
    height = total.shape[0] // len(order)
    middle = len(order) // 2
    for i, pattern in enumerate(order):
        out = keep if i < middle else send
        at = i % middle
        out[at * height : (at + 1) * height, :] = total[pattern * height : (pattern + 1) * height]


def join_kernel(*refs):
    *parts, out = refs
    at = 0
    for part in parts:
        out[at : at + part.shape[0], :] = part[...]
        at += part.shape[0]


def join(*parts):
    return pl.pallas_call(
        join_kernel,
        out_shape=shape(sum(part.shape[0] for part in parts), parts[0].shape[1]),
        in_specs=[vmem()] * len(parts),
        out_specs=vmem(),
        compiler_params=params(4),
        name="join",
    )(*parts)


def gather_rows(block, exp_count):
    found = {0: block}
    found.update({pattern: swap(block, "exp", pattern) for pattern in range(2, exp_count, 2)})
    found.update({pattern ^ 1: swap(piece, "exp", 1) for pattern, piece in list(found.items())})
    return [found[pattern] for pattern in range(exp_count)]


def add(a, b):
    return (a.astype(F32) + b.astype(F32)).astype(BF16)


def sum_of(a, b):
    return a.astype(F32) + b.astype(F32)


def local(attn_part, resid, refusal, norm_gain, route_ids, gate_q, w_gate, w_up, w_down):
    tp_count = lax.axis_size("tp")
    exp_count = lax.axis_size("exp")
    rows, cols = resid.shape
    full = refusal.shape[0]
    local_experts, _, hidden = w_gate.shape
    experts = local_experts * exp_count
    tail = -(-(experts + PARTS) // LANES) * LANES
    total_rows = rows * exp_count
    me = lax.axis_index("tp").astype(jnp.int32).reshape(1)
    first = (lax.axis_index("exp") * local_experts).astype(jnp.int32).reshape(1)
    me, first = lax.optimization_barrier((me, first))
    core, orders = exp_bits(exp_count)
    refusal = refusal.reshape(1, full)

    *slices, base, share, unit = pl.pallas_call(
        cut_kernel,
        out_shape=[shape(rows, cols + LANES)] * (tp_count - 1)
        + [shape(rows, cols, dtype=F32), shape(rows, LANES, dtype=F32), shape(1, cols, dtype=F32)],
        in_specs=[smem()] + [pl.BlockSpec(memory_space=pltpu.HBM)] * 3,
        out_specs=[vmem()] * (tp_count + 2),
        scratch_shapes=[
            pltpu.VMEM((rows, full), BF16),
            pltpu.VMEM((rows, cols), BF16),
            pltpu.VMEM((1, full), F32),
            pltpu.SemaphoreType.DMA((3,)),
        ],
        compiler_params=params(4),
        name="cut_heads",
    )(me, off_chip(attn_part[0]), off_chip(resid), off_chip(refusal))
    parts = [swap(value, "tp", k + 1) for k, value in enumerate(slices)]

    message, projected = pl.pallas_call(
        functools.partial(project_kernel, experts),
        out_shape=[shape(rows, cols + tail), shape(rows, cols, dtype=F32)],
        in_specs=[vmem()] * (5 + tp_count),
        out_specs=[vmem()] * 2,
        compiler_params=params(4),
        name="project",
    )(base, share, unit, norm_gain.reshape(1, cols), route_ids, gate_q, *parts)

    groups = [join(message, swap(message, "tp", 1))]
    bit = 2
    while bit < tp_count:
        groups.append(swap(groups[0] if bit == 2 else join(*groups), "tp", bit))
        bit *= 2

    state, held_down = [], {}
    sizes = [group.shape[0] // rows for group in groups]
    starts = [0] + sizes[1:]
    for i, group in enumerate(groups):
        pieces = gather_rows(group, exp_count)
        chunks, flip = sizes[i], starts[i]
        ahead, columns = starts[-1 - i], sizes[-1 - i] * cols
        start, last = i == 0, i == len(groups) - 1
        down_shape = pltpu.VMEM((local_experts, hidden, columns), BF16)
        acc = pltpu.VMEM((local_experts, total_rows, hidden), F32)
        if last:
            out_shape = [shape(total_rows, local_experts * hidden), down_shape]
            out_specs = [pl.BlockSpec((total_rows, hidden), lambda e, *_: (0, e)), vmem()]
        else:
            out_shape = [acc, acc, pltpu.VMEM((total_rows, tail), F32), down_shape]
            out_specs = [vmem()] * 4
        weights = [off_chip(w_gate), off_chip(w_up)]
        specs = [
            pl.BlockSpec(
                (1, chunks * cols, hidden),
                lambda e, me, first, flip=flip, chunks=chunks: (e, (me[0] ^ flip) // chunks, 0),
            )
        ] * 2
        scratch = [pltpu.VMEM((total_rows, chunks * cols), BF16)]
        *state, held_down[ahead] = pl.pallas_call(
            functools.partial(up_kernel, start, last, chunks, ahead, full, experts),
            out_shape=out_shape,
            grid_spec=pltpu.PrefetchScalarGridSpec(
                num_scalar_prefetch=2,
                grid=(local_experts,),
                in_specs=specs + [pl.BlockSpec(memory_space=pltpu.HBM)] + [vmem()] * (len(pieces) + len(state)),
                out_specs=out_specs,
                scratch_shapes=scratch
                + ([pltpu.VMEM((total_rows, tail), F32)] if last else [])
                + [pltpu.SemaphoreType.DMA(())],
            ),
            input_output_aliases={} if start or last else {5 + len(pieces) + j: j for j in range(3)},
            compiler_params=params(22),
            cost_estimate=pl.CostEstimate(
                flops=4 * total_rows * chunks * cols * hidden * local_experts,
                bytes_accessed=4 * chunks * cols * hidden * local_experts,
                transcendentals=0,
            ),
            name="gate_up",
        )(me, first, *weights, off_chip(w_down), *pieces, *[on_chip(v) for v in state])
    activation = state[0]

    steps = 2 if cols % (2 * LANES) == 0 else 1
    width = cols // steps
    results, gates_open = {}, []
    for k in reversed(range(tp_count)):
        order = orders[k % 2]
        block = max(place for place in held_down if place <= k)
        source = activation
        if len(gates_open) > 1:
            source, _ = lax.optimization_barrier((activation, gates_open[-2]))
        keep, send = pl.pallas_call(
            functools.partial(down_kernel, relative_order([core] + order), k, cols),
            out_shape=[shape(total_rows // 2, cols)] * 2,
            grid_spec=pltpu.PrefetchScalarGridSpec(
                num_scalar_prefetch=1,
                grid=(steps,),
                in_specs=[vmem()] * 2,
                out_specs=[pl.BlockSpec((total_rows // 2, width), lambda i, me: (0, i))] * 2,
            ),
            compiler_params=params(8),
            cost_estimate=pl.CostEstimate(
                flops=2 * total_rows * cols * hidden * local_experts,
                bytes_accessed=2 * cols * hidden * local_experts,
                transcendentals=0,
            ),
            name="down",
        )(me, source, on_chip(held_down[block]))
        mine, theirs = keep, swap(send, "exp", core)
        for i, bit in enumerate(order):
            middle = mine.shape[0] // 2
            away = add(mine[middle:], theirs[middle:])
            if i == 0:
                gates_open.append(away)
            mine, theirs = add(mine[:middle], theirs[:middle]), swap(away, "exp", bit)
        results[k] = (mine, theirs)

    bit = tp_count // 2
    while bit:
        far = jnp.concatenate([functools.reduce(sum_of, results[k]) for k in range(bit, 2 * bit)], axis=0)
        got = swap(far.astype(BF16), "tp", bit)
        for k in range(bit):
            results[k] = results[k] + (got[k * rows : (k + 1) * rows],)
        bit //= 2
    return (projected + functools.reduce(sum_of, results[0])).astype(BF16)


def solution(mesh):
    return jax.shard_map(
        local,
        mesh=mesh,
        in_specs=(
            P("tp", "exp", None),
            P("exp", "tp"),
            P(),
            P("tp"),
            P("exp", None),
            P("exp", None),
            P("exp", None, "tp"),
            P("exp", None, "tp"),
            P("exp", "tp", None),
        ),
        out_specs=P("exp", "tp"),
        check_vma=False,
    )
```

```python
import functools
import jax
import jax.numpy as jnp
from jax import lax
from jax.experimental import pallas as pl
from jax.experimental.pallas import tpu as pltpu
from jax.sharding import PartitionSpec as P

EPSILON = 1e-06
GATE_UNIT = 128.0
LANES = 128
PARTS = 3
F32 = jnp.float32
BF16 = jnp.bfloat16


def vmem():
    return pl.BlockSpec(memory_space=pltpu.VMEM)


def smem():
    return pl.BlockSpec(memory_space=pltpu.SMEM)


def on_chip(value):
    return pltpu.with_memory_space_constraint(value, pltpu.VMEM)


def off_chip(value):
    return pltpu.with_memory_space_constraint(value, pltpu.HBM)


def params(mib):
    return pltpu.CompilerParams(vmem_limit_bytes=mib << 20)


def shape(*dims, dtype=BF16):
    return jax.ShapeDtypeStruct(dims, dtype)


def swap(value, axis, bit):
    count = lax.axis_size(axis)
    return lax.ppermute(value, axis, [(i, i ^ bit) for i in range(count)])


def exp_bits(exp_count):
    plane = [1 << i for i in range(1, exp_count.bit_length() - 1)]
    x_bits, y_bits = plane[: len(plane) // 2], plane[len(plane) // 2 :]
    return 1, (x_bits + y_bits, y_bits + x_bits)


def relative_order(bits):
    order = [0]
    for bit in reversed(bits):
        order = order + [pattern ^ bit for pattern in order]
    return order


def three_parts(value):
    first = value.astype(BF16).astype(F32)
    second = (value - first).astype(BF16).astype(F32)
    return first, second, (value - first - second).astype(BF16).astype(F32)


def cut_kernel(me, attn_hbm, resid_hbm, refusal_hbm, *refs):
    slices, (base, share, unit, attn, resid, refusal, sems) = refs[:-7], refs[-7:]
    copies = [
        pltpu.make_async_copy(source, target, sems.at[i])
        for i, (source, target) in enumerate(((attn_hbm, attn), (resid_hbm, resid), (refusal_hbm, refusal)))
    ]
    for copy in copies:
        copy.start()
    for copy in copies:
        copy.wait()
    rows, width = resid.shape
    scale = lax.rsqrt(jnp.sum(refusal[...] * refusal[...]) + EPSILON)
    own = refusal[:, pl.ds(pl.multiple_of(me[0] * width, LANES), width)] * scale
    unit[...] = own
    total = jnp.sum(attn[...].astype(F32) * (refusal[...] * scale), axis=1, keepdims=True)
    total = total + jnp.sum(resid[...].astype(F32) * own, axis=1, keepdims=True)
    share[...] = jnp.broadcast_to(total, share.shape)
    lane = lax.broadcasted_iota(jnp.int32, share.shape, 1)
    tail = jnp.zeros(share.shape, F32)
    for i, part in enumerate(three_parts(total)):
        tail = jnp.where(lane == i, part, tail)
    tail = tail.astype(BF16)
    for i, out in enumerate(slices):
        out[:, :width] = attn[:, pl.ds(pl.multiple_of((me[0] ^ (i + 1)) * width, LANES), width)]
        out[:, width:] = tail
    here = attn[:, pl.ds(pl.multiple_of(me[0] * width, LANES), width)]
    base[...] = resid[...].astype(F32) + here.astype(F32)


def project_kernel(experts, base, share, unit, gain, ids, gates, *refs):
    parts, (message, projected) = refs[:-2], refs[-2:]
    rows, width = base.shape
    total, along = base[...], share[:, :1]
    for part in parts:
        total = total + part[:, :width].astype(F32)
        along = along + jnp.sum(part[:, width:].astype(F32), axis=1, keepdims=True)
    value = total - along * unit[...]
    projected[...] = value
    message[:, :width] = (value * gain[...]).astype(BF16)
    lane = lax.broadcasted_iota(jnp.int32, (rows, message.shape[1] - width), 1)
    tail = jnp.zeros(lane.shape, F32)
    for i in range(ids.shape[1]):
        tail = tail + jnp.where(ids[:, i : i + 1] == lane, gates[:, i : i + 1].astype(F32), 0.0)
    tail = tail / GATE_UNIT
    for i, part in enumerate(three_parts(jnp.sum(value * value, axis=1, keepdims=True))):
        tail = jnp.where(lane == experts + i, part, tail)
    message[:, width:] = tail.astype(BF16)


def load_kernel(me, gate_hbm, up_hbm, gate, up, sems):
    depth = gate.shape[1]
    here = pl.ds(pl.multiple_of((me[0] >> 1) * depth, LANES), depth)
    copies = [
        pltpu.make_async_copy(source.at[:, here, :], target, sems.at[i])
        for i, (source, target) in enumerate(((gate_hbm, gate), (up_hbm, up)))
    ]
    for copy in copies:
        copy.start()
    for copy in copies:
        copy.wait()


def up_kernel(start, last, chunks, ahead, full, experts, me, first, w_gate, w_up, down_hbm, *refs):
    *refs, sem = refs
    x = refs[-1 - last]
    held_down = refs[-2 - last]
    if last:
        out, side = refs[-4], refs[-1]
        pieces, (gate_in, up_in, side_in) = refs[:-7], refs[-7:-4]
    else:
        gate_acc, up_acc, side = refs[-5:-2]
        pieces = refs[:-5] if start else refs[:-8]
    expert = pl.program_id(0)
    columns = held_down.shape[2]
    block = me[0] ^ ahead
    copy = pltpu.make_async_copy(
        down_hbm.at[:, :, pl.ds(pl.multiple_of(block * columns, LANES), columns)], held_down, sem
    )
    width = x.shape[1] // chunks

    @pl.when(expert == (0 if start or down_hbm.shape[0] == 1 else 1))
    def _():
        copy.start()

    @pl.when(expert == 0)
    def _():
        height = pieces[0].shape[0] // chunks
        for i, piece in enumerate(pieces):
            there = slice(i * height, (i + 1) * height)
            for j in range(chunks):
                here = slice(j * height, (j + 1) * height)
                slot = (me[0] & (chunks - 1)) ^ j
                x[there, pl.ds(pl.multiple_of(slot * width, LANES), width)] = piece[here, :width]
                tail = piece[here, width:].astype(F32)
                lane = lax.broadcasted_iota(jnp.int32, tail.shape, 1)
                if j or not start:
                    before = side_in if last and not j else side
                    tail = before[there, :] + jnp.where(lane >= experts, tail, 0.0)
                side[there, :] = tail

    gate = jnp.dot(x[...], w_gate[expert if start else 0], preferred_element_type=F32)
    up = jnp.dot(x[...], w_up[expert if start else 0], preferred_element_type=F32)
    if start:
        gate_acc[expert] = gate
        up_acc[expert] = up
    elif not last:
        gate_acc[expert] += gate
        up_acc[expert] += up
    else:
        beside = side[...]
        lane = lax.broadcasted_iota(jnp.int32, beside.shape, 1)
        weight = jnp.sum(jnp.where(lane == first[0] + expert, beside, 0.0), axis=1, keepdims=True)
        square = jnp.sum(jnp.where(lane >= experts, beside, 0.0), axis=1, keepdims=True)
        inverse = lax.rsqrt(square / full + EPSILON)
        gate = (gate_in[expert] + gate) * inverse
        up = (up_in[expert] + up) * inverse
        out[...] = (jax.nn.silu(gate) * up * weight).astype(BF16)

    @pl.when(expert == pl.num_programs(0) - 1)
    def _():
        copy.wait()


def down_kernel(order, ahead, me, activation, w_down, *refs):
    if ahead is None:
        keep, send = refs
    else:
        down_hbm, keep, send, held_down, sem = refs
        columns = held_down.shape[2]
        there = pl.ds(pl.multiple_of((me[0] ^ ahead) * columns, LANES), columns)
        copy = pltpu.make_async_copy(down_hbm.at[:, :, there], held_down, sem)

        @pl.when(pl.program_id(0) == 0)
        def _():
            copy.start()

    width = keep.shape[1]
    here = pl.ds(pl.multiple_of(pl.program_id(0) * width, LANES), width)
    weights = w_down[:, :, here].reshape(-1, width)
    total = jnp.dot(activation[...], weights, preferred_element_type=F32).astype(BF16)
    height = total.shape[0] // len(order)
    middle = len(order) // 2
    for i, pattern in enumerate(order):
        out = keep if i < middle else send
        at = i % middle
        out[at * height : (at + 1) * height, :] = total[pattern * height : (pattern + 1) * height]
    if ahead is not None:

        @pl.when(pl.program_id(0) == pl.num_programs(0) - 1)
        def _():
            copy.wait()


def join_kernel(*refs):
    *parts, out = refs
    at = 0
    for part in parts:
        out[at : at + part.shape[0], :] = part[...]
        at += part.shape[0]


def join(*parts):
    return pl.pallas_call(
        join_kernel,
        out_shape=shape(sum(part.shape[0] for part in parts), parts[0].shape[1]),
        in_specs=[vmem()] * len(parts),
        out_specs=vmem(),
        compiler_params=params(4),
        name="join",
    )(*parts)


def after(value, *others):
    return lax.optimization_barrier((value, *others))[0]


def cross_plane(block, exp_count):
    found = {0: block}
    found.update({pattern: swap(block, "exp", pattern) for pattern in range(2, exp_count, 2)})
    return found


def cross_core(found):
    both = dict(found)
    both.update({pattern ^ 1: swap(piece, "exp", 1) for pattern, piece in found.items()})
    return [both[pattern] for pattern in sorted(both)]


def add(a, b):
    return (a.astype(F32) + b.astype(F32)).astype(BF16)


def sum_of(a, b):
    return a.astype(F32) + b.astype(F32)


def local(attn_part, resid, refusal, norm_gain, route_ids, gate_q, w_gate, w_up, w_down):
    tp_count = lax.axis_size("tp")
    exp_count = lax.axis_size("exp")
    rows, cols = resid.shape
    full = refusal.shape[0]
    local_experts, _, hidden = w_gate.shape
    experts = local_experts * exp_count
    tail = -(-(experts + PARTS) // LANES) * LANES
    total_rows = rows * exp_count
    me = lax.axis_index("tp").astype(jnp.int32).reshape(1)
    first = (lax.axis_index("exp") * local_experts).astype(jnp.int32).reshape(1)
    me, first = lax.optimization_barrier((me, first))
    core, orders = exp_bits(exp_count)
    refusal = refusal.reshape(1, full)

    *slices, base, share, unit = pl.pallas_call(
        cut_kernel,
        out_shape=[shape(rows, cols + LANES)] * (tp_count - 1)
        + [shape(rows, cols, dtype=F32), shape(rows, LANES, dtype=F32), shape(1, cols, dtype=F32)],
        in_specs=[smem()] + [pl.BlockSpec(memory_space=pltpu.HBM)] * 3,
        out_specs=[vmem()] * (tp_count + 2),
        scratch_shapes=[
            pltpu.VMEM((rows, full), BF16),
            pltpu.VMEM((rows, cols), BF16),
            pltpu.VMEM((1, full), F32),
            pltpu.SemaphoreType.DMA((3,)),
        ],
        compiler_params=params(4),
        name="cut_heads",
    )(me, off_chip(attn_part[0]), off_chip(resid), off_chip(refusal))
    parts = [swap(value, "tp", k + 1) for k, value in enumerate(slices)]

    message, projected = pl.pallas_call(
        functools.partial(project_kernel, experts),
        out_shape=[shape(rows, cols + tail), shape(rows, cols, dtype=F32)],
        in_specs=[vmem()] * (5 + tp_count),
        out_specs=[vmem()] * 2,
        compiler_params=params(4),
        name="project",
    )(base, share, unit, norm_gain.reshape(1, cols), route_ids, gate_q, *parts)

    groups = [join(message, swap(message, "tp", 1))]
    bit = 2
    while bit < tp_count:
        groups.append(swap(groups[0] if bit == 2 else join(*groups), "tp", bit))
        bit *= 2

    plane = cross_plane(groups[0], exp_count)
    held_gate, held_up = pl.pallas_call(
        load_kernel,
        out_shape=[pltpu.VMEM((local_experts, 2 * cols, hidden), BF16)] * 2,
        in_specs=[smem()] + [pl.BlockSpec(memory_space=pltpu.HBM)] * 2,
        out_specs=[vmem()] * 2,
        scratch_shapes=[pltpu.SemaphoreType.DMA((2,))],
        compiler_params=params(8),
        cost_estimate=pl.CostEstimate(flops=0, bytes_accessed=8 * cols * hidden * local_experts, transcendentals=0),
        name="load_weights",
    )(after(me, plane[exp_count - 2]), off_chip(w_gate), off_chip(w_up))
    plane[2] = after(plane[2], held_gate)

    state, held_down = [], {}
    places = list(reversed(range(tp_count)))
    sizes = [group.shape[0] // rows for group in groups]
    starts = [0] + sizes[1:]
    for i, group in enumerate(groups):
        if i:
            plane = cross_plane(group, exp_count)
            plane = {pattern: after(piece, state[-1]) for pattern, piece in plane.items()}
        pieces = cross_core(plane)
        chunks, flip = sizes[i], starts[i]
        ahead = places[i]
        start, last = i == 0, i == len(groups) - 1
        down_shape = pltpu.VMEM((local_experts, hidden, cols), BF16)
        acc = pltpu.VMEM((local_experts, total_rows, hidden), F32)
        if last:
            out_shape = [shape(total_rows, local_experts * hidden), down_shape]
            out_specs = [pl.BlockSpec((total_rows, hidden), lambda e, *_: (0, e)), vmem()]
        else:
            out_shape = [acc, acc, pltpu.VMEM((total_rows, tail), F32), down_shape]
            out_specs = [vmem()] * 4
        weights = [on_chip(held_gate), on_chip(held_up)] if i == 0 else [off_chip(w_gate), off_chip(w_up)]
        specs = [
            pl.BlockSpec(
                (1, chunks * cols, hidden),
                lambda e, me, first, flip=flip, chunks=chunks: (e, (me[0] ^ flip) // chunks, 0),
            )
        ] * 2
        if i == 0:
            specs = [vmem()] * 2
        scratch = [pltpu.VMEM((total_rows, chunks * cols), BF16)]
        *state, held_down[ahead] = pl.pallas_call(
            functools.partial(up_kernel, start, last, chunks, ahead, full, experts),
            out_shape=out_shape,
            grid_spec=pltpu.PrefetchScalarGridSpec(
                num_scalar_prefetch=2,
                grid=(local_experts,),
                in_specs=specs + [pl.BlockSpec(memory_space=pltpu.HBM)] + [vmem()] * (len(pieces) + len(state)),
                out_specs=out_specs,
                scratch_shapes=scratch
                + ([pltpu.VMEM((total_rows, tail), F32)] if last else [])
                + [pltpu.SemaphoreType.DMA(())],
            ),
            input_output_aliases={} if start or last else {5 + len(pieces) + j: j for j in range(3)},
            compiler_params=params(6 if start else 22),
            cost_estimate=pl.CostEstimate(
                flops=4 * total_rows * chunks * cols * hidden * local_experts,
                bytes_accessed=4 * chunks * cols * hidden * local_experts,
                transcendentals=0,
            ),
            name="gate_up",
        )(me, first, *weights, off_chip(w_down), *pieces, *[on_chip(v) for v in state])
    activation = state[0]

    steps = 2 if cols % (2 * LANES) == 0 else 1
    width = cols // steps
    stages = len(orders[0]) + 1
    events = [(float(j), 0, j, None) for j in range(tp_count)]
    events += [(j + 1.5 + 2 * stage, stage, j, stage) for j in range(tp_count) for stage in range(stages)]
    mine, theirs, opened, done = {}, {}, [], []
    for _, _, j, stage in sorted(events, key=lambda event: event[:3]):
        k = places[j]
        order = orders[k % 2]
        if stage is None:
            ahead = places[j + len(groups)] if j + len(groups) < tp_count else None
            held = [] if ahead is None else [pltpu.VMEM((local_experts, hidden, cols), BF16)]
            keep, send, *found = pl.pallas_call(
                functools.partial(down_kernel, relative_order([core] + order), ahead),
                out_shape=[shape(total_rows // 2, cols)] * 2 + held,
                grid_spec=pltpu.PrefetchScalarGridSpec(
                    num_scalar_prefetch=1,
                    grid=(steps,),
                    in_specs=[vmem()] * 2 + [pl.BlockSpec(memory_space=pltpu.HBM)] * len(held),
                    out_specs=[pl.BlockSpec((total_rows // 2, width), lambda i, me: (0, i))] * 2 + [vmem()] * len(held),
                    scratch_shapes=[pltpu.SemaphoreType.DMA(())] * len(held),
                ),
                compiler_params=params(8),
                cost_estimate=pl.CostEstimate(
                    flops=2 * total_rows * cols * hidden * local_experts,
                    bytes_accessed=2 * cols * hidden * local_experts,
                    transcendentals=0,
                ),
                name="down",
            )(me, after(activation, *opened[-1:]), on_chip(held_down[k]), *[off_chip(w_down)] * len(held))
            if found:
                held_down[ahead] = found[0]
            mine[k], theirs[k] = keep, swap(send, "exp", core)
        elif stage < stages - 1:
            middle = mine[k].shape[0] // 2
            got = after(theirs[k], *opened[-1:])
            away = add(mine[k][middle:], got[middle:])
            opened.append(away)
            mine[k], theirs[k] = add(mine[k][:middle], got[:middle]), swap(away, "exp", order[stage])
        elif k:
            away = add(mine[k], after(theirs[k], *opened[-1:]))
            opened.append(away)
            done.append(swap(away, "tp", k))
        else:
            done += [mine[k], theirs[k]]
    return functools.reduce(sum_of, [projected] + done).astype(BF16)


def solution(mesh):
    return jax.shard_map(
        local,
        mesh=mesh,
        in_specs=(
            P("tp", "exp", None),
            P("exp", "tp"),
            P(),
            P("tp"),
            P("exp", None),
            P("exp", None),
            P("exp", None, "tp"),
            P("exp", None, "tp"),
            P("exp", "tp", None),
        ),
        out_specs=P("exp", "tp"),
        check_vma=False,
    )
```

```python
import functools
import jax
import jax.numpy as jnp
from jax import lax
from jax.experimental import pallas as pl
from jax.experimental.pallas import tpu as pltpu
from jax.sharding import PartitionSpec as P

EPSILON = 1e-06
GATE_UNIT = 128.0
LANES = 128
PARTS = 3
F32 = jnp.float32
BF16 = jnp.bfloat16


def vmem():
    return pl.BlockSpec(memory_space=pltpu.VMEM)


def smem():
    return pl.BlockSpec(memory_space=pltpu.SMEM)


def on_chip(value):
    return pltpu.with_memory_space_constraint(value, pltpu.VMEM)


def off_chip(value):
    return pltpu.with_memory_space_constraint(value, pltpu.HBM)


def params(mib):
    return pltpu.CompilerParams(vmem_limit_bytes=mib << 20)


def shape(*dims, dtype=BF16):
    return jax.ShapeDtypeStruct(dims, dtype)


def swap(value, axis, bit):
    count = lax.axis_size(axis)
    return lax.ppermute(value, axis, [(i, i ^ bit) for i in range(count)])


def exp_bits(exp_count):
    plane = [1 << i for i in range(1, exp_count.bit_length() - 1)]
    x_bits, y_bits = plane[: len(plane) // 2], plane[len(plane) // 2 :]
    return 1, (x_bits + y_bits, y_bits + x_bits)


def relative_order(bits):
    order = [0]
    for bit in reversed(bits):
        order = order + [pattern ^ bit for pattern in order]
    return order


def three_parts(value):
    first = value.astype(BF16).astype(F32)
    second = (value - first).astype(BF16).astype(F32)
    return first, second, (value - first - second).astype(BF16).astype(F32)


def cut_kernel(me, attn_hbm, resid_hbm, refusal_hbm, *refs):
    slices, (base, share, unit, attn, resid, refusal, sems) = refs[:-7], refs[-7:]
    copies = [
        pltpu.make_async_copy(source, target, sems.at[i])
        for i, (source, target) in enumerate(((attn_hbm, attn), (resid_hbm, resid), (refusal_hbm, refusal)))
    ]
    for copy in copies:
        copy.start()
    for copy in copies:
        copy.wait()
    rows, width = resid.shape
    scale = lax.rsqrt(jnp.sum(refusal[...] * refusal[...]) + EPSILON)
    own = refusal[:, pl.ds(pl.multiple_of(me[0] * width, LANES), width)] * scale
    unit[...] = own
    total = jnp.sum(attn[...].astype(F32) * (refusal[...] * scale), axis=1, keepdims=True)
    total = total + jnp.sum(resid[...].astype(F32) * own, axis=1, keepdims=True)
    share[...] = jnp.broadcast_to(total, share.shape)
    lane = lax.broadcasted_iota(jnp.int32, share.shape, 1)
    tail = jnp.zeros(share.shape, F32)
    for i, part in enumerate(three_parts(total)):
        tail = jnp.where(lane == i, part, tail)
    tail = tail.astype(BF16)
    for i, out in enumerate(slices):
        out[:, :width] = attn[:, pl.ds(pl.multiple_of((me[0] ^ (i + 1)) * width, LANES), width)]
        out[:, width:] = tail
    here = attn[:, pl.ds(pl.multiple_of(me[0] * width, LANES), width)]
    base[...] = resid[...].astype(F32) + here.astype(F32)


def project_kernel(experts, base, share, unit, gain, ids, gates, *refs):
    parts, (message, projected) = refs[:-2], refs[-2:]
    rows, width = base.shape
    total, along = base[...], share[:, :1]
    for part in parts:
        total = total + part[:, :width].astype(F32)
        along = along + jnp.sum(part[:, width:].astype(F32), axis=1, keepdims=True)
    value = total - along * unit[...]
    projected[...] = value
    message[:, :width] = (value * gain[...]).astype(BF16)
    lane = lax.broadcasted_iota(jnp.int32, (rows, message.shape[1] - width), 1)
    tail = jnp.zeros(lane.shape, F32)
    for i in range(ids.shape[1]):
        tail = tail + jnp.where(ids[:, i : i + 1] == lane, gates[:, i : i + 1].astype(F32), 0.0)
    tail = tail / GATE_UNIT
    for i, part in enumerate(three_parts(jnp.sum(value * value, axis=1, keepdims=True))):
        tail = jnp.where(lane == experts + i, part, tail)
    message[:, width:] = tail.astype(BF16)


def copies_of(source, target, sems, block, axis, experts):
    size = target.shape[1 + axis]
    there = pl.ds(pl.multiple_of(block * size, LANES), size)
    place = (there, slice(None)) if axis == 0 else (slice(None), there)
    return [pltpu.make_async_copy(source.at[(e, *place)], target.at[e], sems.at[e]) for e in experts]


def load_kernel(me, hbm, held, sems):
    copies = copies_of(hbm, held, sems, me[0] >> 1, 0, range(held.shape[0]))
    for copy in copies:
        copy.start()
    for copy in copies:
        copy.wait()


def up_kernel(start, last, held, late, refill, chunks, ahead, full, experts, me, first, gate_hbm, up_hbm, down_hbm, *refs):
    refs = list(refs)
    sems = refs.pop()
    side_scratch = refs.pop() if last else None
    x = refs.pop()
    held_down = refs.pop()
    if held:
        w_up, w_gate = refs.pop(), refs.pop()
    if last:
        out, side = refs.pop(), side_scratch
    else:
        side, up_acc, gate_acc = refs.pop(), refs.pop(), refs.pop()
    if not start:
        side_in, up_in, gate_in = refs.pop(), refs.pop(), refs.pop()
    if held:
        refs = refs[2:]
    else:
        w_gate, w_up, *refs = refs
    pieces = refs
    expert = pl.program_id(0)
    count = down_hbm.shape[0]
    width = x.shape[1] // chunks
    down = copies_of(down_hbm, held_down, sems.at[0], me[0] ^ ahead, 1, range(count))

    def rows_of(flip, some):
        block = (me[0] ^ flip) // chunks
        return copies_of(gate_hbm, w_gate, sems.at[1], block, 0, some) + copies_of(up_hbm, w_up, sems.at[2], block, 0, some)

    @pl.when(expert == 0)
    def _():
        if late:
            for copy in rows_of(chunks, [count - 1]):
                copy.start()
        for copy in down:
            copy.start()
        height = pieces[0].shape[0] // chunks
        for i, piece in enumerate(pieces):
            there = slice(i * height, (i + 1) * height)
            for j in range(chunks):
                here = slice(j * height, (j + 1) * height)
                slot = (me[0] & (chunks - 1)) ^ j
                x[there, pl.ds(pl.multiple_of(slot * width, LANES), width)] = piece[here, :width]
                tail = piece[here, width:].astype(F32)
                lane = lax.broadcasted_iota(jnp.int32, tail.shape, 1)
                if j or not start:
                    before = side_in if last and not j else side
                    tail = before[there, :] + jnp.where(lane >= experts, tail, 0.0)
                side[there, :] = tail

    if late:

        @pl.when(expert == count - 1)
        def _():
            for copy in rows_of(chunks, [count - 1]):
                copy.wait()

    if refill:
        for e in range(count - 1):

            @pl.when(expert == e + 1)
            def _():
                for copy in rows_of(chunks, [e]):
                    copy.start()

    here = expert if held else 0
    gate = jnp.dot(x[...], w_gate[here], preferred_element_type=F32)
    up = jnp.dot(x[...], w_up[here], preferred_element_type=F32)
    if start:
        gate_acc[expert] = gate
        up_acc[expert] = up
    elif not last:
        gate_acc[expert] += gate
        up_acc[expert] += up
    else:
        beside = side[...]
        lane = lax.broadcasted_iota(jnp.int32, beside.shape, 1)
        weight = jnp.sum(jnp.where(lane == first[0] + expert, beside, 0.0), axis=1, keepdims=True)
        square = jnp.sum(jnp.where(lane >= experts, beside, 0.0), axis=1, keepdims=True)
        inverse = lax.rsqrt(square / full + EPSILON)
        gate = (gate_in[expert] + gate) * inverse
        up = (up_in[expert] + up) * inverse
        out[...] = (jax.nn.silu(gate) * up * weight).astype(BF16)

    @pl.when(expert == count - 1)
    def _():
        for copy in down + (rows_of(chunks, range(count - 1)) if refill else []):
            copy.wait()


def down_kernel(order, ahead, me, activation, w_down, *refs):
    if ahead is None:
        keep, send = refs
    else:
        down_hbm, keep, send, held_down, sems = refs
        copies = copies_of(down_hbm, held_down, sems, me[0] ^ ahead, 1, range(held_down.shape[0]))

        @pl.when(pl.program_id(0) == 0)
        def _():
            for copy in copies:
                copy.start()

    width = keep.shape[1]
    here = pl.ds(pl.multiple_of(pl.program_id(0) * width, LANES), width)
    weights = w_down[:, :, here].reshape(-1, width)
    total = jnp.dot(activation[...], weights, preferred_element_type=F32).astype(BF16)
    height = total.shape[0] // len(order)
    middle = len(order) // 2
    for i, pattern in enumerate(order):
        out = keep if i < middle else send
        at = i % middle
        out[at * height : (at + 1) * height, :] = total[pattern * height : (pattern + 1) * height]
    if ahead is not None:

        @pl.when(pl.program_id(0) == pl.num_programs(0) - 1)
        def _():
            for copy in copies:
                copy.wait()


def join_kernel(*refs):
    *parts, out = refs
    at = 0
    for part in parts:
        out[at : at + part.shape[0], :] = part[...]
        at += part.shape[0]


def join(*parts):
    return pl.pallas_call(
        join_kernel,
        out_shape=shape(sum(part.shape[0] for part in parts), parts[0].shape[1]),
        in_specs=[vmem()] * len(parts),
        out_specs=vmem(),
        compiler_params=params(4),
        name="join",
    )(*parts)


def after(value, *others):
    return lax.optimization_barrier((value, *others))[0]


def cross_plane(block, exp_count):
    found = {0: block}
    found.update({pattern: swap(block, "exp", pattern) for pattern in range(2, exp_count, 2)})
    return found


def cross_core(found):
    both = dict(found)
    both.update({pattern ^ 1: swap(piece, "exp", 1) for pattern, piece in found.items()})
    return [both[pattern] for pattern in sorted(both)]


def add(a, b):
    return (a.astype(F32) + b.astype(F32)).astype(BF16)


def sum_of(a, b):
    return a.astype(F32) + b.astype(F32)


def local(attn_part, resid, refusal, norm_gain, route_ids, gate_q, w_gate, w_up, w_down):
    tp_count = lax.axis_size("tp")
    exp_count = lax.axis_size("exp")
    rows, cols = resid.shape
    full = refusal.shape[0]
    local_experts, _, hidden = w_gate.shape
    experts = local_experts * exp_count
    tail = -(-(experts + PARTS) // LANES) * LANES
    total_rows = rows * exp_count
    me = lax.axis_index("tp").astype(jnp.int32).reshape(1)
    first = (lax.axis_index("exp") * local_experts).astype(jnp.int32).reshape(1)
    me, first = lax.optimization_barrier((me, first))
    core, orders = exp_bits(exp_count)
    refusal = refusal.reshape(1, full)

    *slices, base, share, unit = pl.pallas_call(
        cut_kernel,
        out_shape=[shape(rows, cols + LANES)] * (tp_count - 1)
        + [shape(rows, cols, dtype=F32), shape(rows, LANES, dtype=F32), shape(1, cols, dtype=F32)],
        in_specs=[smem()] + [pl.BlockSpec(memory_space=pltpu.HBM)] * 3,
        out_specs=[vmem()] * (tp_count + 2),
        scratch_shapes=[
            pltpu.VMEM((rows, full), BF16),
            pltpu.VMEM((rows, cols), BF16),
            pltpu.VMEM((1, full), F32),
            pltpu.SemaphoreType.DMA((3,)),
        ],
        compiler_params=params(4),
        name="cut_heads",
    )(me, off_chip(attn_part[0]), off_chip(resid), off_chip(refusal))
    parts = [swap(value, "tp", k + 1) for k, value in enumerate(slices)]

    def load(source, at):
        return pl.pallas_call(
            load_kernel,
            out_shape=pltpu.VMEM((local_experts, 2 * cols, hidden), BF16),
            in_specs=[smem(), pl.BlockSpec(memory_space=pltpu.HBM)],
            out_specs=vmem(),
            scratch_shapes=[pltpu.SemaphoreType.DMA((local_experts,))],
            compiler_params=params(8),
            cost_estimate=pl.CostEstimate(flops=0, bytes_accessed=4 * cols * hidden * local_experts, transcendentals=0),
            name="load_rows",
        )(at, off_chip(source))

    held_gate = load(w_gate, after(me, share))
    base = after(base, held_gate)

    message, projected = pl.pallas_call(
        functools.partial(project_kernel, experts),
        out_shape=[shape(rows, cols + tail), shape(rows, cols, dtype=F32)],
        in_specs=[vmem()] * (5 + tp_count),
        out_specs=[vmem()] * 2,
        compiler_params=params(4),
        name="project",
    )(base, share, unit, norm_gain.reshape(1, cols), route_ids, gate_q, *parts)

    groups = [join(message, swap(message, "tp", 1))]
    bit = 2
    while bit < tp_count:
        groups.append(swap(groups[0] if bit == 2 else join(*groups), "tp", bit))
        bit *= 2
    sizes = [group.shape[0] // rows for group in groups]
    starts = [0] + sizes[1:]

    plane = cross_plane(groups[0], exp_count)
    held_up = load(w_up, after(me, groups[0]))
    groups[1:] = [after(group, held_up) for group in groups[1:]]
    plane = {pattern: after(piece, groups[-1]) if pattern else piece for pattern, piece in plane.items()}

    state, held_down = [], {}
    places = list(reversed(range(tp_count)))
    for i, group in enumerate(groups):
        if i:
            plane = cross_plane(group, exp_count)
            plane = {pattern: after(piece, state[-1]) for pattern, piece in plane.items()}
        pieces = cross_core(plane)
        chunks, flip = sizes[i], starts[i]
        ahead = places[i]
        start, last = i == 0, i == len(groups) - 1
        down_shape = pltpu.VMEM((local_experts, hidden, cols), BF16)
        acc = pltpu.VMEM((local_experts, total_rows, hidden), F32)
        held = i == 0 or chunks == sizes[i - 1]
        late = held and i > 0
        refill = held and not late and not last and sizes[i + 1] == chunks
        if last:
            out_shape = [shape(total_rows, local_experts * hidden)]
            out_specs = [pl.BlockSpec((total_rows, hidden), lambda e, *_: (0, e))]
        else:
            out_shape = [acc, acc, pltpu.VMEM((total_rows, tail), F32)]
            out_specs = [vmem()] * 3
        weights = [on_chip(held_gate), on_chip(held_up)] if held else [w_gate, w_up]
        specs = [vmem()] * 2
        if not held:
            specs = [
                pl.BlockSpec(
                    (1, chunks * cols, hidden),
                    lambda e, me, first, flip=flip, chunks=chunks: (e, (me[0] ^ flip) // chunks, 0),
                )
            ] * 2
        aliases = {} if start or last else {7 + len(pieces) + j: j for j in range(3)}
        if held:
            aliases.update({5: len(out_shape), 6: len(out_shape) + 1})
            out_shape += [pltpu.VMEM((local_experts, chunks * cols, hidden), BF16)] * 2
            out_specs += [vmem()] * 2
        found = pl.pallas_call(
            functools.partial(up_kernel, start, last, held, late, refill, chunks, ahead, full, experts),
            out_shape=out_shape + [down_shape],
            grid_spec=pltpu.PrefetchScalarGridSpec(
                num_scalar_prefetch=2,
                grid=(local_experts,),
                in_specs=[pl.BlockSpec(memory_space=pltpu.HBM)] * 3 + specs + [vmem()] * (len(pieces) + len(state)),
                out_specs=out_specs + [vmem()],
                scratch_shapes=[pltpu.VMEM((total_rows, chunks * cols), BF16)]
                + ([pltpu.VMEM((total_rows, tail), F32)] if last else [])
                + [pltpu.SemaphoreType.DMA((3, local_experts))],
            ),
            input_output_aliases=aliases,
            compiler_params=params(6 if held else 22),
            cost_estimate=pl.CostEstimate(
                flops=4 * total_rows * chunks * cols * hidden * local_experts,
                bytes_accessed=4 * chunks * cols * hidden * local_experts,
                transcendentals=0,
            ),
            name="gate_up",
        )(
            *(me, first, off_chip(w_gate), off_chip(w_up), off_chip(w_down)),
            *weights,
            *pieces,
            *[on_chip(v) for v in state],
        )
        held_down[ahead] = found[-1]
        if held:
            held_gate, held_up = found[-3:-1]
        state = found[: 1 if last else 3]
    activation = state[0]

    steps = 2 if cols % (2 * LANES) == 0 else 1
    width = cols // steps
    stages = len(orders[0]) + 1
    events = [(float(j), j, None) for j in range(tp_count)]
    events += [(j + 1.5 + 2 * stage, j, stage) for j in range(tp_count) for stage in range(stages)]
    mine, theirs, opened, done = {}, {}, [], []
    for _, j, stage in sorted(events, key=lambda event: event[:2]):
        k = places[j]
        order = orders[k % 2]
        if stage is None:
            ahead = places[j + len(groups)] if j + len(groups) < tp_count else None
            held = [] if ahead is None else [pltpu.VMEM((local_experts, hidden, cols), BF16)]
            keep, send, *found = pl.pallas_call(
                functools.partial(down_kernel, relative_order([core] + order), ahead),
                out_shape=[shape(total_rows // 2, cols)] * 2 + held,
                grid_spec=pltpu.PrefetchScalarGridSpec(
                    num_scalar_prefetch=1,
                    grid=(steps,),
                    in_specs=[vmem()] * 2 + [pl.BlockSpec(memory_space=pltpu.HBM)] * len(held),
                    out_specs=[pl.BlockSpec((total_rows // 2, width), lambda i, me: (0, i))] * 2 + [vmem()] * len(held),
                    scratch_shapes=[pltpu.SemaphoreType.DMA((local_experts,))] * len(held),
                ),
                compiler_params=params(8),
                cost_estimate=pl.CostEstimate(
                    flops=2 * total_rows * cols * hidden * local_experts,
                    bytes_accessed=2 * cols * hidden * local_experts,
                    transcendentals=0,
                ),
                name="down",
            )(me, after(activation, *opened[-1:]), on_chip(held_down[k]), *[off_chip(w_down)] * len(held))
            if found:
                held_down[ahead] = found[0]
            mine[k], theirs[k] = keep, swap(send, "exp", core)
        elif stage < stages - 1:
            middle = mine[k].shape[0] // 2
            got = after(theirs[k], *opened[-1:])
            away = add(mine[k][middle:], got[middle:])
            opened.append(away)
            mine[k], theirs[k] = add(mine[k][:middle], got[:middle]), swap(away, "exp", order[stage])
        elif k:
            away = add(mine[k], after(theirs[k], *opened[-1:]))
            opened.append(away)
            done.append(swap(away, "tp", k))
        else:
            done += [mine[k], theirs[k]]
    return functools.reduce(sum_of, [projected] + done).astype(BF16)


def solution(mesh):
    return jax.shard_map(
        local,
        mesh=mesh,
        in_specs=(
            P("tp", "exp", None),
            P("exp", "tp"),
            P(),
            P("tp"),
            P("exp", None),
            P("exp", None),
            P("exp", None, "tp"),
            P("exp", None, "tp"),
            P("exp", "tp", None),
        ),
        out_specs=P("exp", "tp"),
        check_vma=False,
    )
```

```python
import functools
import jax
import jax.numpy as jnp
from jax import lax
from jax.experimental import pallas as pl
from jax.experimental.pallas import tpu as pltpu
from jax.sharding import PartitionSpec as P

EPSILON = 1e-06
GATE_UNIT = 128.0
LANES = 128
PARTS = 3
F32 = jnp.float32
BF16 = jnp.bfloat16


def vmem():
    return pl.BlockSpec(memory_space=pltpu.VMEM)


def smem():
    return pl.BlockSpec(memory_space=pltpu.SMEM)


def on_chip(value):
    return pltpu.with_memory_space_constraint(value, pltpu.VMEM)


def off_chip(value):
    return pltpu.with_memory_space_constraint(value, pltpu.HBM)


def params(mib):
    return pltpu.CompilerParams(vmem_limit_bytes=mib << 20)


def shape(*dims, dtype=BF16):
    return jax.ShapeDtypeStruct(dims, dtype)


def swap(value, axis, bit):
    count = lax.axis_size(axis)
    return lax.ppermute(value, axis, [(i, i ^ bit) for i in range(count)])


def exp_bits(exp_count):
    plane = [1 << i for i in range(1, exp_count.bit_length() - 1)]
    x_bits, y_bits = plane[: len(plane) // 2], plane[len(plane) // 2 :]
    return 1, (x_bits + y_bits, y_bits + x_bits)


def relative_order(bits):
    order = [0]
    for bit in reversed(bits):
        order = order + [pattern ^ bit for pattern in order]
    return order


def three_parts(value):
    first = value.astype(BF16).astype(F32)
    second = (value - first).astype(BF16).astype(F32)
    return first, second, (value - first - second).astype(BF16).astype(F32)


def cut_kernel(me, attn_hbm, resid_hbm, refusal_hbm, *refs):
    slices, (base, share, unit, attn, resid, refusal, sems) = refs[:-7], refs[-7:]
    copies = [
        pltpu.make_async_copy(source, target, sems.at[i])
        for i, (source, target) in enumerate(((attn_hbm, attn), (resid_hbm, resid), (refusal_hbm, refusal)))
    ]
    for copy in copies:
        copy.start()
    for copy in copies:
        copy.wait()
    rows, width = resid.shape
    scale = lax.rsqrt(jnp.sum(refusal[...] * refusal[...]) + EPSILON)
    own = refusal[:, pl.ds(pl.multiple_of(me[0] * width, LANES), width)] * scale
    unit[...] = own
    total = jnp.sum(attn[...].astype(F32) * (refusal[...] * scale), axis=1, keepdims=True)
    total = total + jnp.sum(resid[...].astype(F32) * own, axis=1, keepdims=True)
    share[...] = jnp.broadcast_to(total, share.shape)
    lane = lax.broadcasted_iota(jnp.int32, share.shape, 1)
    tail = jnp.zeros(share.shape, F32)
    for i, part in enumerate(three_parts(total)):
        tail = jnp.where(lane == i, part, tail)
    tail = tail.astype(BF16)
    for i, out in enumerate(slices):
        out[:, :width] = attn[:, pl.ds(pl.multiple_of((me[0] ^ (i + 1)) * width, LANES), width)]
        out[:, width:] = tail
    here = attn[:, pl.ds(pl.multiple_of(me[0] * width, LANES), width)]
    base[...] = resid[...].astype(F32) + here.astype(F32)


def project_kernel(experts, base, share, unit, gain, ids, gates, *refs):
    parts, (message, projected) = refs[:-2], refs[-2:]
    rows, width = base.shape
    total, along = base[...], share[:, :1]
    for part in parts:
        total = total + part[:, :width].astype(F32)
        along = along + jnp.sum(part[:, width:].astype(F32), axis=1, keepdims=True)
    value = total - along * unit[...]
    projected[...] = value
    message[:, :width] = (value * gain[...]).astype(BF16)
    lane = lax.broadcasted_iota(jnp.int32, (rows, message.shape[1] - width), 1)
    tail = jnp.zeros(lane.shape, F32)
    for i in range(ids.shape[1]):
        tail = tail + jnp.where(ids[:, i : i + 1] == lane, gates[:, i : i + 1].astype(F32), 0.0)
    tail = tail / GATE_UNIT
    for i, part in enumerate(three_parts(jnp.sum(value * value, axis=1, keepdims=True))):
        tail = jnp.where(lane == experts + i, part, tail)
    message[:, width:] = tail.astype(BF16)


def copies_of(source, target, sems, block, axis, experts):
    size = target.shape[1 + axis]
    there = pl.ds(pl.multiple_of(block * size, LANES), size)
    place = (there, slice(None)) if axis == 0 else (slice(None), there)
    return [pltpu.make_async_copy(source.at[(e, *place)], target.at[e], sems.at[e]) for e in experts]


def load_kernel(me, hbm, held, sems):
    copies = copies_of(hbm, held, sems, me[0] >> 1, 0, range(held.shape[0]))
    for copy in copies:
        copy.start()
    for copy in copies:
        copy.wait()


def up_kernel(start, last, held, late, refill, chunks, ahead, full, experts, me, first, gate_hbm, up_hbm, down_hbm, *refs):
    refs = list(refs)
    sems = refs.pop()
    side_scratch = refs.pop() if last else None
    x = refs.pop()
    held_down = [refs.pop() for _ in ahead][::-1]
    if held:
        w_up, w_gate = refs.pop(), refs.pop()
    if last:
        out, side = refs.pop(), side_scratch
    else:
        side, up_acc, gate_acc = refs.pop(), refs.pop(), refs.pop()
    if not start:
        side_in, up_in, gate_in = refs.pop(), refs.pop(), refs.pop()
    if held:
        refs = refs[2:]
    else:
        w_gate, w_up, *refs = refs
    pieces = refs
    expert = pl.program_id(0)
    count = down_hbm.shape[0]
    width = x.shape[1] // chunks
    down = []
    for i, (place, target) in enumerate(zip(ahead, held_down)):
        down += copies_of(down_hbm, target, sems.at[2 + i], me[0] ^ place, 1, range(count))

    def rows_of(flip, some):
        block = (me[0] ^ flip) // chunks
        return copies_of(gate_hbm, w_gate, sems.at[0], block, 0, some) + copies_of(up_hbm, w_up, sems.at[1], block, 0, some)

    @pl.when(expert == 0)
    def _():
        if late:
            for copy in rows_of(chunks, [count - 1]):
                copy.start()
        for copy in down:
            copy.start()
        height = pieces[0].shape[0] // chunks
        for i, piece in enumerate(pieces):
            there = slice(i * height, (i + 1) * height)
            for j in range(chunks):
                here = slice(j * height, (j + 1) * height)
                slot = (me[0] & (chunks - 1)) ^ j
                x[there, pl.ds(pl.multiple_of(slot * width, LANES), width)] = piece[here, :width]
                tail = piece[here, width:].astype(F32)
                lane = lax.broadcasted_iota(jnp.int32, tail.shape, 1)
                if j or not start:
                    before = side_in if last and not j else side
                    tail = before[there, :] + jnp.where(lane >= experts, tail, 0.0)
                side[there, :] = tail

    if late:

        @pl.when(expert == count - 1)
        def _():
            for copy in rows_of(chunks, [count - 1]):
                copy.wait()

    if refill:
        for e in range(count - 1):

            @pl.when(expert == e + 1)
            def _():
                for copy in rows_of(chunks, [e]):
                    copy.start()

    here = expert if held else 0
    gate = jnp.dot(x[...], w_gate[here], preferred_element_type=F32)
    up = jnp.dot(x[...], w_up[here], preferred_element_type=F32)
    if start:
        gate_acc[expert] = gate
        up_acc[expert] = up
    elif not last:
        gate_acc[expert] += gate
        up_acc[expert] += up
    else:
        beside = side[...]
        lane = lax.broadcasted_iota(jnp.int32, beside.shape, 1)
        weight = jnp.sum(jnp.where(lane == first[0] + expert, beside, 0.0), axis=1, keepdims=True)
        square = jnp.sum(jnp.where(lane >= experts, beside, 0.0), axis=1, keepdims=True)
        inverse = lax.rsqrt(square / full + EPSILON)
        gate = (gate_in[expert] + gate) * inverse
        up = (up_in[expert] + up) * inverse
        out[...] = (jax.nn.silu(gate) * up * weight).astype(BF16)

    @pl.when(expert == count - 1)
    def _():
        for copy in down + (rows_of(chunks, range(count - 1)) if refill else []):
            copy.wait()


def down_kernel(order, ahead, me, activation, w_down, *refs):
    if ahead is None:
        keep, send = refs
    else:
        down_hbm, keep, send, held_down, sems = refs
        copies = copies_of(down_hbm, held_down, sems, me[0] ^ ahead, 1, range(held_down.shape[0]))

        @pl.when(pl.program_id(0) == 0)
        def _():
            for copy in copies:
                copy.start()

    width = keep.shape[1]
    here = pl.ds(pl.multiple_of(pl.program_id(0) * width, LANES), width)
    weights = w_down[:, :, here].reshape(-1, width)
    total = jnp.dot(activation[...], weights, preferred_element_type=F32).astype(BF16)
    height = total.shape[0] // len(order)
    middle = len(order) // 2
    for i, pattern in enumerate(order):
        out = keep if i < middle else send
        at = i % middle
        out[at * height : (at + 1) * height, :] = total[pattern * height : (pattern + 1) * height]
    if ahead is not None:

        @pl.when(pl.program_id(0) == pl.num_programs(0) - 1)
        def _():
            for copy in copies:
                copy.wait()


def join_kernel(*refs):
    *parts, out = refs
    at = 0
    for part in parts:
        out[at : at + part.shape[0], :] = part[...]
        at += part.shape[0]


def join(*parts):
    return pl.pallas_call(
        join_kernel,
        out_shape=shape(sum(part.shape[0] for part in parts), parts[0].shape[1]),
        in_specs=[vmem()] * len(parts),
        out_specs=vmem(),
        compiler_params=params(4),
        name="join",
    )(*parts)


def after(value, *others):
    return lax.optimization_barrier((value, *others))[0]


def cross_plane(block, exp_count):
    found = {0: block}
    found.update({pattern: swap(block, "exp", pattern) for pattern in range(2, exp_count, 2)})
    return found


def cross_core(found):
    both = dict(found)
    both.update({pattern ^ 1: swap(piece, "exp", 1) for pattern, piece in found.items()})
    return [both[pattern] for pattern in sorted(both)]


def add(a, b):
    return (a.astype(F32) + b.astype(F32)).astype(BF16)


def sum_of(a, b):
    return a.astype(F32) + b.astype(F32)


def local(attn_part, resid, refusal, norm_gain, route_ids, gate_q, w_gate, w_up, w_down):
    tp_count = lax.axis_size("tp")
    exp_count = lax.axis_size("exp")
    rows, cols = resid.shape
    full = refusal.shape[0]
    local_experts, _, hidden = w_gate.shape
    experts = local_experts * exp_count
    tail = -(-(experts + PARTS) // LANES) * LANES
    total_rows = rows * exp_count
    me = lax.axis_index("tp").astype(jnp.int32).reshape(1)
    first = (lax.axis_index("exp") * local_experts).astype(jnp.int32).reshape(1)
    me, first = lax.optimization_barrier((me, first))
    core, orders = exp_bits(exp_count)
    refusal = refusal.reshape(1, full)

    *slices, base, share, unit = pl.pallas_call(
        cut_kernel,
        out_shape=[shape(rows, cols + LANES)] * (tp_count - 1)
        + [shape(rows, cols, dtype=F32), shape(rows, LANES, dtype=F32), shape(1, cols, dtype=F32)],
        in_specs=[smem()] + [pl.BlockSpec(memory_space=pltpu.HBM)] * 3,
        out_specs=[vmem()] * (tp_count + 2),
        scratch_shapes=[
            pltpu.VMEM((rows, full), BF16),
            pltpu.VMEM((rows, cols), BF16),
            pltpu.VMEM((1, full), F32),
            pltpu.SemaphoreType.DMA((3,)),
        ],
        compiler_params=params(4),
        name="cut_heads",
    )(me, off_chip(attn_part[0]), off_chip(resid), off_chip(refusal))
    parts = [swap(value, "tp", k + 1) for k, value in enumerate(slices)]

    def load(source, at):
        return pl.pallas_call(
            load_kernel,
            out_shape=pltpu.VMEM((local_experts, 2 * cols, hidden), BF16),
            in_specs=[smem(), pl.BlockSpec(memory_space=pltpu.HBM)],
            out_specs=vmem(),
            scratch_shapes=[pltpu.SemaphoreType.DMA((local_experts,))],
            compiler_params=params(8),
            cost_estimate=pl.CostEstimate(flops=0, bytes_accessed=4 * cols * hidden * local_experts, transcendentals=0),
            name="load_rows",
        )(at, off_chip(source))

    held_gate = load(w_gate, after(me, share))
    base = after(base, held_gate)

    message, projected = pl.pallas_call(
        functools.partial(project_kernel, experts),
        out_shape=[shape(rows, cols + tail), shape(rows, cols, dtype=F32)],
        in_specs=[vmem()] * (5 + tp_count),
        out_specs=[vmem()] * 2,
        compiler_params=params(4),
        name="project",
    )(base, share, unit, norm_gain.reshape(1, cols), route_ids, gate_q, *parts)

    groups = [join(message, swap(message, "tp", 1))]
    bit = 2
    while bit < tp_count:
        groups.append(swap(groups[0] if bit == 2 else join(*groups), "tp", bit))
        bit *= 2
    sizes = [group.shape[0] // rows for group in groups]
    starts = [0] + sizes[1:]

    plane = cross_plane(groups[0], exp_count)
    held_up = load(w_up, after(me, groups[0]))
    groups[1:] = [after(group, held_up) for group in groups[1:]]
    plane = {pattern: after(piece, groups[-1]) if pattern else piece for pattern, piece in plane.items()}

    state, held_down = [], {}
    places = list(reversed(range(tp_count)))
    for i, group in enumerate(groups):
        if i:
            plane = cross_plane(group, exp_count)
            plane = {pattern: after(piece, state[-1]) for pattern, piece in plane.items()}
        pieces = cross_core(plane)
        chunks, flip = sizes[i], starts[i]
        ahead = places[i : i + 1]
        start, last = i == 0, i == len(groups) - 1
        down_shape = pltpu.VMEM((local_experts, hidden, cols), BF16)
        acc = pltpu.VMEM((local_experts, total_rows, hidden), F32)
        held = i == 0 or chunks == sizes[i - 1]
        late = held and i > 0
        refill = held and not late and not last and sizes[i + 1] == chunks
        if last:
            out_shape = [shape(total_rows, local_experts * hidden)]
            out_specs = [pl.BlockSpec((total_rows, hidden), lambda e, *_: (0, e))]
        else:
            out_shape = [acc, acc, pltpu.VMEM((total_rows, tail), F32)]
            out_specs = [vmem()] * 3
        weights = [on_chip(held_gate), on_chip(held_up)] if held else [w_gate, w_up]
        specs = [vmem()] * 2
        if not held:
            specs = [
                pl.BlockSpec(
                    (1, chunks * cols, hidden),
                    lambda e, me, first, flip=flip, chunks=chunks: (e, (me[0] ^ flip) // chunks, 0),
                )
            ] * 2
        aliases = {} if start or last else {7 + len(pieces) + j: j for j in range(3)}
        if held:
            aliases.update({5: len(out_shape), 6: len(out_shape) + 1})
            out_shape += [pltpu.VMEM((local_experts, chunks * cols, hidden), BF16)] * 2
            out_specs += [vmem()] * 2
        found = pl.pallas_call(
            functools.partial(up_kernel, start, last, held, late, refill, chunks, ahead, full, experts),
            out_shape=out_shape + [down_shape] * len(ahead),
            grid_spec=pltpu.PrefetchScalarGridSpec(
                num_scalar_prefetch=2,
                grid=(local_experts,),
                in_specs=[pl.BlockSpec(memory_space=pltpu.HBM)] * 3 + specs + [vmem()] * (len(pieces) + len(state)),
                out_specs=out_specs + [vmem()] * len(ahead),
                scratch_shapes=[pltpu.VMEM((total_rows, chunks * cols), BF16)]
                + ([pltpu.VMEM((total_rows, tail), F32)] if last else [])
                + [pltpu.SemaphoreType.DMA((2 + len(ahead), local_experts))],
            ),
            input_output_aliases=aliases,
            compiler_params=params(6 if held else 22),
            cost_estimate=pl.CostEstimate(
                flops=4 * total_rows * chunks * cols * hidden * local_experts,
                bytes_accessed=4 * chunks * cols * hidden * local_experts,
                transcendentals=0,
            ),
            name="gate_up",
        )(
            *(me, first, off_chip(w_gate), off_chip(w_up), off_chip(w_down)),
            *weights,
            *pieces,
            *[on_chip(v) for v in state],
        )
        held_down.update(zip(ahead, found[-len(ahead) :]))
        if held:
            held_gate, held_up = found[len(out_shape) - 2 : len(out_shape)]
        state = found[: 1 if last else 3]
    activation = state[0]

    steps = 2 if cols % (2 * LANES) == 0 else 1
    width = cols // steps
    stages = len(orders[0]) + 1
    pairs = [(low, low + 1) for low in range(0, tp_count, 2)]
    events, open_stage = [], {}
    for n, pair in enumerate(pairs):
        events += [(j, None) for j in pair]
        for before in pairs[:n]:
            open_stage[before] += 1
            events += [(j, open_stage[before]) for j in before if open_stage[before] < stages]
        events += [(j, 0) for j in pair]
        open_stage[pair] = 0
    for _ in range(stages):
        for pair in pairs:
            open_stage[pair] += 1
            events += [(j, open_stage[pair]) for j in pair if open_stage[pair] < stages]
    mine, theirs, opened, done = {}, {}, [], []
    for j, stage in events:
        k = places[j]
        order = orders[k % 2]
        if stage is None:
            ahead = next((p for p in places[: j + 3 - j % 2] if p not in held_down), None)
            held = [] if ahead is None else [pltpu.VMEM((local_experts, hidden, cols), BF16)]
            keep, send, *found = pl.pallas_call(
                functools.partial(down_kernel, relative_order([core] + order), ahead),
                out_shape=[shape(total_rows // 2, cols)] * 2 + held,
                grid_spec=pltpu.PrefetchScalarGridSpec(
                    num_scalar_prefetch=1,
                    grid=(steps,),
                    in_specs=[vmem()] * 2 + [pl.BlockSpec(memory_space=pltpu.HBM)] * len(held),
                    out_specs=[pl.BlockSpec((total_rows // 2, width), lambda i, me: (0, i))] * 2 + [vmem()] * len(held),
                    scratch_shapes=[pltpu.SemaphoreType.DMA((local_experts,))] * len(held),
                ),
                compiler_params=params(8),
                cost_estimate=pl.CostEstimate(
                    flops=2 * total_rows * cols * hidden * local_experts,
                    bytes_accessed=2 * cols * hidden * local_experts,
                    transcendentals=0,
                ),
                name="down",
            )(me, after(activation, *opened[-1:]), on_chip(held_down[k]), *[off_chip(w_down)] * len(held))
            if found:
                held_down[ahead] = found[0]
            mine[k], theirs[k] = keep, swap(send, "exp", core)
        elif stage < stages - 1:
            middle = mine[k].shape[0] // 2
            got = after(theirs[k], *opened[-1:])
            away = add(mine[k][middle:], got[middle:])
            opened.append(away)
            mine[k], theirs[k] = add(mine[k][:middle], got[:middle]), swap(away, "exp", order[stage])
        elif k:
            away = add(mine[k], after(theirs[k], *opened[-1:]))
            opened.append(away)
            done.append(swap(away, "tp", k))
        else:
            done += [mine[k], theirs[k]]
    return functools.reduce(sum_of, [projected] + done).astype(BF16)


def solution(mesh):
    return jax.shard_map(
        local,
        mesh=mesh,
        in_specs=(
            P("tp", "exp", None),
            P("exp", "tp"),
            P(),
            P("tp"),
            P("exp", None),
            P("exp", None),
            P("exp", None, "tp"),
            P("exp", None, "tp"),
            P("exp", "tp", None),
        ),
        out_specs=P("exp", "tp"),
        check_vma=False,
    )
```

```python
import functools
import jax
import jax.numpy as jnp
from jax import lax
from jax.experimental import pallas as pl
from jax.experimental.pallas import tpu as pltpu
from jax.sharding import PartitionSpec as P

EPSILON = 1e-06
GATE_UNIT = 128.0
LANES = 128
PARTS = 3
F32 = jnp.float32
BF16 = jnp.bfloat16


def vmem():
    return pl.BlockSpec(memory_space=pltpu.VMEM)


def smem():
    return pl.BlockSpec(memory_space=pltpu.SMEM)


def on_chip(value):
    return pltpu.with_memory_space_constraint(value, pltpu.VMEM)


def off_chip(value):
    return pltpu.with_memory_space_constraint(value, pltpu.HBM)


def params(mib):
    return pltpu.CompilerParams(vmem_limit_bytes=mib << 20)


def shape(*dims, dtype=BF16):
    return jax.ShapeDtypeStruct(dims, dtype)


def swap(value, axis, bit):
    count = lax.axis_size(axis)
    return lax.ppermute(value, axis, [(i, i ^ bit) for i in range(count)])


def exp_bits(exp_count):
    plane = [1 << i for i in range(1, exp_count.bit_length() - 1)]
    x_bits, y_bits = plane[: len(plane) // 2], plane[len(plane) // 2 :]
    return 1, (x_bits + y_bits, y_bits + x_bits)


def relative_order(bits):
    order = [0]
    for bit in reversed(bits):
        order = order + [pattern ^ bit for pattern in order]
    return order


def three_parts(value):
    first = value.astype(BF16).astype(F32)
    second = (value - first).astype(BF16).astype(F32)
    return first, second, (value - first - second).astype(BF16).astype(F32)


def cut_kernel(me, attn_hbm, resid_hbm, refusal_hbm, *refs):
    slices, (base, share, unit, attn, resid, refusal, sems) = refs[:-7], refs[-7:]
    copies = [
        pltpu.make_async_copy(source, target, sems.at[i])
        for i, (source, target) in enumerate(((attn_hbm, attn), (resid_hbm, resid), (refusal_hbm, refusal)))
    ]
    for copy in copies:
        copy.start()
    for copy in copies:
        copy.wait()
    rows, width = resid.shape
    scale = lax.rsqrt(jnp.sum(refusal[...] * refusal[...]) + EPSILON)
    own = refusal[:, pl.ds(pl.multiple_of(me[0] * width, LANES), width)] * scale
    unit[...] = own
    total = jnp.sum(attn[...].astype(F32) * (refusal[...] * scale), axis=1, keepdims=True)
    total = total + jnp.sum(resid[...].astype(F32) * own, axis=1, keepdims=True)
    share[...] = jnp.broadcast_to(total, share.shape)
    lane = lax.broadcasted_iota(jnp.int32, share.shape, 1)
    tail = jnp.zeros(share.shape, F32)
    for i, part in enumerate(three_parts(total)):
        tail = jnp.where(lane == i, part, tail)
    tail = tail.astype(BF16)
    for i, out in enumerate(slices):
        out[:, :width] = attn[:, pl.ds(pl.multiple_of((me[0] ^ (i + 1)) * width, LANES), width)]
        out[:, width:] = tail
    here = attn[:, pl.ds(pl.multiple_of(me[0] * width, LANES), width)]
    base[...] = resid[...].astype(F32) + here.astype(F32)


def project_kernel(experts, base, share, unit, gain, ids, gates, *refs):
    parts, (message, projected) = refs[:-2], refs[-2:]
    rows, width = base.shape
    total, along = base[...], share[:, :1]
    for part in parts:
        total = total + part[:, :width].astype(F32)
        along = along + jnp.sum(part[:, width:].astype(F32), axis=1, keepdims=True)
    value = total - along * unit[...]
    projected[...] = value
    message[:, :width] = (value * gain[...]).astype(BF16)
    lane = lax.broadcasted_iota(jnp.int32, (rows, message.shape[1] - width), 1)
    tail = jnp.zeros(lane.shape, F32)
    for i in range(ids.shape[1]):
        tail = tail + jnp.where(ids[:, i : i + 1] == lane, gates[:, i : i + 1].astype(F32), 0.0)
    tail = tail / GATE_UNIT
    for i, part in enumerate(three_parts(jnp.sum(value * value, axis=1, keepdims=True))):
        tail = jnp.where(lane == experts + i, part, tail)
    message[:, width:] = tail.astype(BF16)


def copies_of(source, target, sems, block, axis, experts, low=0):
    size = target.shape[1 + axis]
    there = pl.ds(pl.multiple_of(block * size, LANES), size)
    place = (there, slice(None)) if axis == 0 else (slice(None), there)
    return [pltpu.make_async_copy(source.at[(e, *place)], target.at[e - low], sems.at[e]) for e in experts]


def load_kernel(me, hbm, held, sems):
    copies = copies_of(hbm, held, sems, me[0] >> 1, 0, range(held.shape[0]))
    for copy in copies:
        copy.start()
    for copy in copies:
        copy.wait()


def up_kernel(start, last, held, late, refill, chunks, ahead, full, experts, me, first, gate_hbm, up_hbm, down_hbm, *refs):
    refs = list(refs)
    sems = refs.pop()
    side_scratch = refs.pop() if last else None
    x = refs.pop()
    held_down = [refs.pop() for _ in ahead][::-1]
    if held:
        w_up, w_gate = refs.pop(), refs.pop()
    if last:
        out, side = refs.pop(), side_scratch
    else:
        side, up_acc, gate_acc = refs.pop(), refs.pop(), refs.pop()
    if not start:
        side_in, up_in, gate_in = refs.pop(), refs.pop(), refs.pop()
    if held:
        refs = refs[2:]
    else:
        w_gate, w_up, *refs = refs
    pieces = refs
    expert = pl.program_id(0)
    count = down_hbm.shape[0]
    width = x.shape[1] // chunks
    down = []
    for i, ((place, low, high), target) in enumerate(zip(ahead, held_down)):
        down += copies_of(down_hbm, target, sems.at[2 + i], me[0] ^ place, 1, range(low, high), low)

    def rows_of(flip, some):
        block = (me[0] ^ flip) // chunks
        return copies_of(gate_hbm, w_gate, sems.at[0], block, 0, some) + copies_of(up_hbm, w_up, sems.at[1], block, 0, some)

    @pl.when(expert == 0)
    def _():
        if late:
            for copy in rows_of(chunks, [count - 1]):
                copy.start()
        for copy in down:
            copy.start()
        height = pieces[0].shape[0] // chunks
        for i, piece in enumerate(pieces):
            there = slice(i * height, (i + 1) * height)
            for j in range(chunks):
                here = slice(j * height, (j + 1) * height)
                slot = (me[0] & (chunks - 1)) ^ j
                x[there, pl.ds(pl.multiple_of(slot * width, LANES), width)] = piece[here, :width]
                tail = piece[here, width:].astype(F32)
                lane = lax.broadcasted_iota(jnp.int32, tail.shape, 1)
                if j or not start:
                    before = side_in if last and not j else side
                    tail = before[there, :] + jnp.where(lane >= experts, tail, 0.0)
                side[there, :] = tail

    if late:

        @pl.when(expert == count - 1)
        def _():
            for copy in rows_of(chunks, [count - 1]):
                copy.wait()

    if refill:
        for e in range(count - 1):

            @pl.when(expert == e + 1)
            def _():
                for copy in rows_of(chunks, [e]):
                    copy.start()

    here = expert if held else 0
    gate = jnp.dot(x[...], w_gate[here], preferred_element_type=F32)
    up = jnp.dot(x[...], w_up[here], preferred_element_type=F32)
    if start:
        gate_acc[expert] = gate
        up_acc[expert] = up
    elif not last:
        gate_acc[expert] += gate
        up_acc[expert] += up
    else:
        beside = side[...]
        lane = lax.broadcasted_iota(jnp.int32, beside.shape, 1)
        weight = jnp.sum(jnp.where(lane == first[0] + expert, beside, 0.0), axis=1, keepdims=True)
        square = jnp.sum(jnp.where(lane >= experts, beside, 0.0), axis=1, keepdims=True)
        inverse = lax.rsqrt(square / full + EPSILON)
        gate = (gate_in[expert] + gate) * inverse
        up = (up_in[expert] + up) * inverse
        out[...] = (jax.nn.silu(gate) * up * weight).astype(BF16)

    @pl.when(expert == count - 1)
    def _():
        for copy in down + (rows_of(chunks, range(count - 1)) if refill else []):
            copy.wait()


def down_kernel(order, ranges, ahead, me, activation, *refs):
    parts, refs = refs[: len(ranges)], refs[len(ranges) :]
    if not ahead:
        keep, send = refs
    else:
        down_hbm, keep, send, *held_down, sems = refs
        copies = []
        for i, ((place, low, high), target) in enumerate(zip(ahead, held_down)):
            copies += copies_of(down_hbm, target, sems.at[i], me[0] ^ place, 1, range(low, high), low)

        @pl.when(pl.program_id(0) == 0)
        def _():
            for copy in copies:
                copy.start()

    width = keep.shape[1]
    hidden = parts[0].shape[1]
    here = pl.ds(pl.multiple_of(pl.program_id(0) * width, LANES), width)
    total = 0.0
    for (low, high), part in zip(ranges, parts):
        weights = part[:, :, here].reshape(-1, width)
        total = total + jnp.dot(activation[:, low * hidden : high * hidden], weights, preferred_element_type=F32)
    total = total.astype(BF16)
    height = total.shape[0] // len(order)
    middle = len(order) // 2
    for i, pattern in enumerate(order):
        out = keep if i < middle else send
        at = i % middle
        out[at * height : (at + 1) * height, :] = total[pattern * height : (pattern + 1) * height]
    if ahead:

        @pl.when(pl.program_id(0) == pl.num_programs(0) - 1)
        def _():
            for copy in copies:
                copy.wait()


def join_kernel(*refs):
    *parts, out = refs
    at = 0
    for part in parts:
        out[at : at + part.shape[0], :] = part[...]
        at += part.shape[0]


def join(*parts):
    return pl.pallas_call(
        join_kernel,
        out_shape=shape(sum(part.shape[0] for part in parts), parts[0].shape[1]),
        in_specs=[vmem()] * len(parts),
        out_specs=vmem(),
        compiler_params=params(4),
        name="join",
    )(*parts)


def after(value, *others):
    return lax.optimization_barrier((value, *others))[0]


def cross_plane(block, exp_count):
    found = {0: block}
    found.update({pattern: swap(block, "exp", pattern) for pattern in range(2, exp_count, 2)})
    return found


def cross_core(found):
    both = dict(found)
    both.update({pattern ^ 1: swap(piece, "exp", 1) for pattern, piece in found.items()})
    return [both[pattern] for pattern in sorted(both)]


def add(a, b):
    return (a.astype(F32) + b.astype(F32)).astype(BF16)


def sum_of(a, b):
    return a.astype(F32) + b.astype(F32)


def local(attn_part, resid, refusal, norm_gain, route_ids, gate_q, w_gate, w_up, w_down):
    tp_count = lax.axis_size("tp")
    exp_count = lax.axis_size("exp")
    rows, cols = resid.shape
    full = refusal.shape[0]
    local_experts, _, hidden = w_gate.shape
    experts = local_experts * exp_count
    tail = -(-(experts + PARTS) // LANES) * LANES
    total_rows = rows * exp_count
    small = 4 * max(1, total_rows // 256)
    me = lax.axis_index("tp").astype(jnp.int32).reshape(1)
    first = (lax.axis_index("exp") * local_experts).astype(jnp.int32).reshape(1)
    me, first = lax.optimization_barrier((me, first))
    core, orders = exp_bits(exp_count)
    refusal = refusal.reshape(1, full)

    *slices, base, share, unit = pl.pallas_call(
        cut_kernel,
        out_shape=[shape(rows, cols + LANES)] * (tp_count - 1)
        + [shape(rows, cols, dtype=F32), shape(rows, LANES, dtype=F32), shape(1, cols, dtype=F32)],
        in_specs=[smem()] + [pl.BlockSpec(memory_space=pltpu.HBM)] * 3,
        out_specs=[vmem()] * (tp_count + 2),
        scratch_shapes=[
            pltpu.VMEM((rows, full), BF16),
            pltpu.VMEM((rows, cols), BF16),
            pltpu.VMEM((1, full), F32),
            pltpu.SemaphoreType.DMA((3,)),
        ],
        compiler_params=params(4),
        name="cut_heads",
    )(me, off_chip(attn_part[0]), off_chip(resid), off_chip(refusal))
    parts = [swap(value, "tp", k + 1) for k, value in enumerate(slices)]

    def load(source, at):
        return pl.pallas_call(
            load_kernel,
            out_shape=pltpu.VMEM((local_experts, 2 * cols, hidden), BF16),
            in_specs=[smem(), pl.BlockSpec(memory_space=pltpu.HBM)],
            out_specs=vmem(),
            scratch_shapes=[pltpu.SemaphoreType.DMA((local_experts,))],
            compiler_params=params(8),
            cost_estimate=pl.CostEstimate(flops=0, bytes_accessed=4 * cols * hidden * local_experts, transcendentals=0),
            name="load_rows",
        )(at, off_chip(source))

    held_gate = load(w_gate, after(me, share))
    base = after(base, held_gate)

    message, projected = pl.pallas_call(
        functools.partial(project_kernel, experts),
        out_shape=[shape(rows, cols + tail), shape(rows, cols, dtype=F32)],
        in_specs=[vmem()] * (5 + tp_count),
        out_specs=[vmem()] * 2,
        compiler_params=params(4),
        name="project",
    )(base, share, unit, norm_gain.reshape(1, cols), route_ids, gate_q, *parts)

    groups = [join(message, swap(message, "tp", 1))]
    bit = 2
    while bit < tp_count:
        groups.append(swap(groups[0] if bit == 2 else join(*groups), "tp", bit))
        bit *= 2
    sizes = [group.shape[0] // rows for group in groups]
    starts = [0] + sizes[1:]

    plane = cross_plane(groups[0], exp_count)
    held_up = load(w_up, after(me, groups[0]))
    groups[1:] = [after(group, held_up) for group in groups[1:]]
    plane = {pattern: after(piece, groups[-1]) if pattern else piece for pattern, piece in plane.items()}

    state, held_down = [], {}
    places = list(reversed(range(tp_count)))
    halves = [(0, local_experts)] if local_experts == 1 else [(0, local_experts // 2), (local_experts // 2, local_experts)]
    units = [(k, low, high) for k in places for low, high in halves]

    def part_of(unit):
        return pltpu.VMEM((unit[2] - unit[1], hidden, cols), BF16)

    for i, group in enumerate(groups):
        if i:
            plane = cross_plane(group, exp_count)
            plane = {pattern: after(piece, state[-1]) for pattern, piece in plane.items()}
        pieces = cross_core(plane)
        chunks, flip = sizes[i], starts[i]
        start, last = i == 0, i == len(groups) - 1
        ahead = units[len(held_down) :][: len(halves)]
        acc = pltpu.VMEM((local_experts, total_rows, hidden), F32)
        held = i == 0 or chunks == sizes[i - 1]
        late = held and i > 0
        refill = held and not late and not last and sizes[i + 1] == chunks
        if last:
            out_shape = [shape(total_rows, local_experts * hidden)]
            out_specs = [pl.BlockSpec((total_rows, hidden), lambda e, *_: (0, e))]
        else:
            out_shape = [acc, acc, pltpu.VMEM((total_rows, tail), F32)]
            out_specs = [vmem()] * 3
        weights = [on_chip(held_gate), on_chip(held_up)] if held else [w_gate, w_up]
        specs = [vmem()] * 2
        if not held:
            specs = [
                pl.BlockSpec(
                    (1, chunks * cols, hidden),
                    lambda e, me, first, flip=flip, chunks=chunks: (e, (me[0] ^ flip) // chunks, 0),
                )
            ] * 2
        aliases = {} if start or last else {7 + len(pieces) + j: j for j in range(3)}
        if held:
            aliases.update({5: len(out_shape), 6: len(out_shape) + 1})
            out_shape += [pltpu.VMEM((local_experts, chunks * cols, hidden), BF16)] * 2
            out_specs += [vmem()] * 2
        found = pl.pallas_call(
            functools.partial(up_kernel, start, last, held, late, refill, chunks, ahead, full, experts),
            out_shape=out_shape + [part_of(unit) for unit in ahead],
            grid_spec=pltpu.PrefetchScalarGridSpec(
                num_scalar_prefetch=2,
                grid=(local_experts,),
                in_specs=[pl.BlockSpec(memory_space=pltpu.HBM)] * 3 + specs + [vmem()] * (len(pieces) + len(state)),
                out_specs=out_specs + [vmem()] * len(ahead),
                scratch_shapes=[pltpu.VMEM((total_rows, chunks * cols), BF16)]
                + ([pltpu.VMEM((total_rows, tail), F32)] if last else [])
                + [pltpu.SemaphoreType.DMA((2 + len(ahead), local_experts))],
            ),
            input_output_aliases=aliases,
            compiler_params=params(small * 3 // 2 if held else 22),
            cost_estimate=pl.CostEstimate(
                flops=4 * total_rows * chunks * cols * hidden * local_experts,
                bytes_accessed=4 * chunks * cols * hidden * local_experts,
                transcendentals=0,
            ),
            name="gate_up",
        )(
            *(me, first, off_chip(w_gate), off_chip(w_up), off_chip(w_down)),
            *weights,
            *pieces,
            *[on_chip(v) for v in state],
        )
        held_down.update(zip(ahead, found[-len(ahead) :]))
        if held:
            held_gate, held_up = found[len(out_shape) - 2 : len(out_shape)]
        state = found[: 1 if last else 3]
    activation = state[0]

    steps = 2 if cols % (2 * LANES) == 0 else 1
    width = cols // steps
    stages = len(orders[0]) + 1
    events = [(0, None)]
    for j in range(1, tp_count):
        events += [(j, None)] + ([(j - 1, 0)] if j < tp_count - 1 else [])
    for turn in range(stages):
        for j in range(tp_count):
            stage = turn + (1 if j < tp_count - 2 else 0)
            events += [(j, stage)] if stage < stages else []
    mine, theirs, opened, done = {}, {}, [], []
    for j, stage in events:
        k = places[j]
        order = orders[k % 2]
        if stage is None:
            ahead = units[len(held_down) :]
            ahead = ahead[: max(1, sum(unit[0] in places[: j + 2] for unit in ahead))]
            held = [part_of(unit) for unit in ahead]
            parts = [on_chip(held_down[(k, low, high)]) for low, high in halves]
            keep, send, *found = pl.pallas_call(
                functools.partial(down_kernel, relative_order([core] + order), halves, ahead),
                out_shape=[shape(total_rows // 2, cols)] * 2 + held,
                grid_spec=pltpu.PrefetchScalarGridSpec(
                    num_scalar_prefetch=1,
                    grid=(steps,),
                    in_specs=[vmem()] * (1 + len(parts)) + [pl.BlockSpec(memory_space=pltpu.HBM)] * bool(held),
                    out_specs=[pl.BlockSpec((total_rows // 2, width), lambda i, me: (0, i))] * 2 + [vmem()] * len(held),
                    scratch_shapes=[pltpu.SemaphoreType.DMA((len(held), local_experts))] * bool(held),
                ),
                compiler_params=params(2 * small),
                cost_estimate=pl.CostEstimate(
                    flops=2 * total_rows * cols * hidden * local_experts,
                    bytes_accessed=2 * cols * hidden * local_experts,
                    transcendentals=0,
                ),
                name="down",
            )(me, after(activation, *opened[-1:]), *parts, *[off_chip(w_down)] * bool(held))
            held_down.update(zip(ahead, found))
            mine[k], theirs[k] = keep, swap(send, "exp", core)
        elif stage < stages - 1:
            middle = mine[k].shape[0] // 2
            got = after(theirs[k], *opened[-1:])
            away = add(mine[k][middle:], got[middle:])
            opened.append(away)
            mine[k], theirs[k] = add(mine[k][:middle], got[:middle]), swap(away, "exp", order[stage])
        elif k:
            away = add(mine[k], after(theirs[k], *opened[-1:]))
            opened.append(away)
            done.append(swap(away, "tp", k))
        else:
            done += [mine[k], theirs[k]]
    return functools.reduce(sum_of, [projected] + done).astype(BF16)


def solution(mesh):
    return jax.shard_map(
        local,
        mesh=mesh,
        in_specs=(
            P("tp", "exp", None),
            P("exp", "tp"),
            P(),
            P("tp"),
            P("exp", None),
            P("exp", None),
            P("exp", None, "tp"),
            P("exp", None, "tp"),
            P("exp", "tp", None),
        ),
        out_specs=P("exp", "tp"),
        check_vma=False,
    )
```

```python
import functools
import jax
import jax.numpy as jnp
from jax import lax
from jax.experimental import pallas as pl
from jax.experimental.pallas import tpu as pltpu
from jax.sharding import PartitionSpec as P

EPSILON = 1e-06
GATE_UNIT = 128.0
LANES = 128
PARTS = 3
F32 = jnp.float32
BF16 = jnp.bfloat16


def vmem():
    return pl.BlockSpec(memory_space=pltpu.VMEM)


def smem():
    return pl.BlockSpec(memory_space=pltpu.SMEM)


def on_chip(value):
    return pltpu.with_memory_space_constraint(value, pltpu.VMEM)


def off_chip(value):
    return pltpu.with_memory_space_constraint(value, pltpu.HBM)


def params(mib):
    return pltpu.CompilerParams(vmem_limit_bytes=mib << 20)


def shape(*dims, dtype=BF16):
    return jax.ShapeDtypeStruct(dims, dtype)


def swap(value, axis, bit):
    count = lax.axis_size(axis)
    return lax.ppermute(value, axis, [(i, i ^ bit) for i in range(count)])


def exp_bits(exp_count):
    plane = [1 << i for i in range(1, exp_count.bit_length() - 1)]
    x_bits, y_bits = plane[: len(plane) // 2], plane[len(plane) // 2 :]
    return 1, (x_bits + y_bits, y_bits + x_bits)


def relative_order(bits):
    order = [0]
    for bit in reversed(bits):
        order = order + [pattern ^ bit for pattern in order]
    return order


def three_parts(value):
    first = value.astype(BF16).astype(F32)
    second = (value - first).astype(BF16).astype(F32)
    return first, second, (value - first - second).astype(BF16).astype(F32)


def cut_kernel(me, attn_hbm, resid_hbm, refusal_hbm, *refs):
    slices, (base, share, unit, attn, resid, refusal, sems) = refs[:-7], refs[-7:]
    copies = [
        pltpu.make_async_copy(source, target, sems.at[i])
        for i, (source, target) in enumerate(((attn_hbm, attn), (resid_hbm, resid), (refusal_hbm, refusal)))
    ]
    for copy in copies:
        copy.start()
    for copy in copies:
        copy.wait()
    rows, width = resid.shape
    scale = lax.rsqrt(jnp.sum(refusal[...] * refusal[...]) + EPSILON)
    own = refusal[:, pl.ds(pl.multiple_of(me[0] * width, LANES), width)] * scale
    unit[...] = own
    total = jnp.sum(attn[...].astype(F32) * (refusal[...] * scale), axis=1, keepdims=True)
    total = total + jnp.sum(resid[...].astype(F32) * own, axis=1, keepdims=True)
    share[...] = jnp.broadcast_to(total, share.shape)
    lane = lax.broadcasted_iota(jnp.int32, share.shape, 1)
    tail = jnp.zeros(share.shape, F32)
    for i, part in enumerate(three_parts(total)):
        tail = jnp.where(lane == i, part, tail)
    tail = tail.astype(BF16)
    for i, out in enumerate(slices):
        out[:, :width] = attn[:, pl.ds(pl.multiple_of((me[0] ^ (i + 1)) * width, LANES), width)]
        out[:, width:] = tail
    here = attn[:, pl.ds(pl.multiple_of(me[0] * width, LANES), width)]
    base[...] = resid[...].astype(F32) + here.astype(F32)


def project_kernel(experts, base, share, unit, gain, ids, gates, *refs):
    parts, (message, projected) = refs[:-2], refs[-2:]
    rows, width = base.shape
    total, along = base[...], share[:, :1]
    for part in parts:
        total = total + part[:, :width].astype(F32)
        along = along + jnp.sum(part[:, width:].astype(F32), axis=1, keepdims=True)
    value = total - along * unit[...]
    projected[...] = value
    message[:, :width] = (value * gain[...]).astype(BF16)
    lane = lax.broadcasted_iota(jnp.int32, (rows, message.shape[1] - width), 1)
    tail = jnp.zeros(lane.shape, F32)
    for i in range(ids.shape[1]):
        tail = tail + jnp.where(ids[:, i : i + 1] == lane, gates[:, i : i + 1].astype(F32), 0.0)
    tail = tail / GATE_UNIT
    for i, part in enumerate(three_parts(jnp.sum(value * value, axis=1, keepdims=True))):
        tail = jnp.where(lane == experts + i, part, tail)
    message[:, width:] = tail.astype(BF16)


def copies_of(source, target, sems, block, axis, experts, low=0):
    size = target.shape[1 + axis]
    there = pl.ds(pl.multiple_of(block * size, LANES), size)
    place = (there, slice(None)) if axis == 0 else (slice(None), there)
    return [pltpu.make_async_copy(source.at[(e, *place)], target.at[e - low], sems.at[e]) for e in experts]


def load_kernel(me, hbm, held, sems):
    copies = copies_of(hbm, held, sems, me[0] >> 1, 0, range(held.shape[0]))
    for copy in copies:
        copy.start()
    for copy in copies:
        copy.wait()


def up_kernel(start, last, held, late, refill, chunks, ahead, full, experts, me, first, gate_hbm, up_hbm, down_hbm, *refs):
    refs = list(refs)
    sems = refs.pop()
    side_scratch = refs.pop() if last else None
    x = refs.pop()
    held_down = [refs.pop() for _ in ahead][::-1]
    if held:
        w_up, w_gate = refs.pop(), refs.pop()
    if last:
        out, side = refs.pop(), side_scratch
    else:
        side, up_acc, gate_acc = refs.pop(), refs.pop(), refs.pop()
    if not start:
        side_in, up_in, gate_in = refs.pop(), refs.pop(), refs.pop()
    if held:
        refs = refs[2:]
    else:
        w_gate, w_up, *refs = refs
    pieces = refs
    expert = pl.program_id(0)
    count = down_hbm.shape[0]
    width = x.shape[1] // chunks
    down = []
    for i, ((place, low, high), target) in enumerate(zip(ahead, held_down)):
        down += copies_of(down_hbm, target, sems.at[2 + i], me[0] ^ place, 1, range(low, high), low)

    def rows_of(flip, some):
        block = (me[0] ^ flip) // chunks
        return copies_of(gate_hbm, w_gate, sems.at[0], block, 0, some) + copies_of(up_hbm, w_up, sems.at[1], block, 0, some)

    @pl.when(expert == 0)
    def _():
        if late:
            for copy in rows_of(chunks, [count - 1]):
                copy.start()
        for copy in down:
            copy.start()
        height = pieces[0].shape[0] // chunks
        for i, piece in enumerate(pieces):
            there = slice(i * height, (i + 1) * height)
            for j in range(chunks):
                here = slice(j * height, (j + 1) * height)
                slot = (me[0] & (chunks - 1)) ^ j
                x[there, pl.ds(pl.multiple_of(slot * width, LANES), width)] = piece[here, :width]
                tail = piece[here, width:].astype(F32)
                lane = lax.broadcasted_iota(jnp.int32, tail.shape, 1)
                if j or not start:
                    before = side_in if last and not j else side
                    tail = before[there, :] + jnp.where(lane >= experts, tail, 0.0)
                side[there, :] = tail

    if late:

        @pl.when(expert == count - 1)
        def _():
            for copy in rows_of(chunks, [count - 1]):
                copy.wait()

    if refill:
        for e in range(count - 1):

            @pl.when(expert == e + 1)
            def _():
                for copy in rows_of(chunks, [e]):
                    copy.start()

    here = expert if held else 0
    gate = jnp.dot(x[...], w_gate[here], preferred_element_type=F32)
    up = jnp.dot(x[...], w_up[here], preferred_element_type=F32)
    if start:
        gate_acc[expert] = gate
        up_acc[expert] = up
    elif not last:
        gate_acc[expert] += gate
        up_acc[expert] += up
    else:
        beside = side[...]
        lane = lax.broadcasted_iota(jnp.int32, beside.shape, 1)
        weight = jnp.sum(jnp.where(lane == first[0] + expert, beside, 0.0), axis=1, keepdims=True)
        square = jnp.sum(jnp.where(lane >= experts, beside, 0.0), axis=1, keepdims=True)
        inverse = lax.rsqrt(square / full + EPSILON)
        gate = (gate_in[expert] + gate) * inverse
        up = (up_in[expert] + up) * inverse
        out[...] = (jax.nn.silu(gate) * up * weight).astype(BF16)

    @pl.when(expert == count - 1)
    def _():
        for copy in down + (rows_of(chunks, range(count - 1)) if refill else []):
            copy.wait()


def down_kernel(order, ranges, ahead, me, activation, *refs):
    parts, refs = refs[: len(ranges)], refs[len(ranges) :]
    if not ahead:
        keep, send = refs
    else:
        down_hbm, keep, send, *held_down, sems = refs
        copies = []
        for i, ((place, low, high), target) in enumerate(zip(ahead, held_down)):
            copies += copies_of(down_hbm, target, sems.at[i], me[0] ^ place, 1, range(low, high), low)

        @pl.when(pl.program_id(0) == 0)
        def _():
            for copy in copies:
                copy.start()

    width = keep.shape[1]
    hidden = parts[0].shape[1]
    here = pl.ds(pl.multiple_of(pl.program_id(0) * width, LANES), width)
    total = 0.0
    for (low, high), part in zip(ranges, parts):
        weights = part[:, :, here].reshape(-1, width)
        total = total + jnp.dot(activation[:, low * hidden : high * hidden], weights, preferred_element_type=F32)
    total = total.astype(BF16)
    height = total.shape[0] // len(order)
    middle = len(order) // 2
    for i, pattern in enumerate(order):
        out = keep if i < middle else send
        at = i % middle
        out[at * height : (at + 1) * height, :] = total[pattern * height : (pattern + 1) * height]
    if ahead:

        @pl.when(pl.program_id(0) == pl.num_programs(0) - 1)
        def _():
            for copy in copies:
                copy.wait()


def join_kernel(*refs):
    *parts, out = refs
    at = 0
    for part in parts:
        out[at : at + part.shape[0], :] = part[...]
        at += part.shape[0]


def join(*parts):
    return pl.pallas_call(
        join_kernel,
        out_shape=shape(sum(part.shape[0] for part in parts), parts[0].shape[1]),
        in_specs=[vmem()] * len(parts),
        out_specs=vmem(),
        compiler_params=params(4),
        name="join",
    )(*parts)


def after(value, *others):
    return lax.optimization_barrier((value, *others))[0]


def cross_plane(block, exp_count):
    found = {0: block}
    found.update({pattern: swap(block, "exp", pattern) for pattern in range(2, exp_count, 2)})
    return found


def cross_core(found):
    both = dict(found)
    both.update({pattern ^ 1: swap(piece, "exp", 1) for pattern, piece in found.items()})
    return [both[pattern] for pattern in sorted(both)]


def add(a, b):
    return (a.astype(F32) + b.astype(F32)).astype(BF16)


def sum_of(a, b):
    return a.astype(F32) + b.astype(F32)


def local(attn_part, resid, refusal, norm_gain, route_ids, gate_q, w_gate, w_up, w_down):
    tp_count = lax.axis_size("tp")
    exp_count = lax.axis_size("exp")
    rows, cols = resid.shape
    full = refusal.shape[0]
    local_experts, _, hidden = w_gate.shape
    experts = local_experts * exp_count
    tail = -(-(experts + PARTS) // LANES) * LANES
    total_rows = rows * exp_count
    small = 4 * max(1, total_rows // 256)
    me = lax.axis_index("tp").astype(jnp.int32).reshape(1)
    first = (lax.axis_index("exp") * local_experts).astype(jnp.int32).reshape(1)
    me, first = lax.optimization_barrier((me, first))
    core, orders = exp_bits(exp_count)
    refusal = refusal.reshape(1, full)

    *slices, base, share, unit = pl.pallas_call(
        cut_kernel,
        out_shape=[shape(rows, cols + LANES)] * (tp_count - 1)
        + [shape(rows, cols, dtype=F32), shape(rows, LANES, dtype=F32), shape(1, cols, dtype=F32)],
        in_specs=[smem()] + [pl.BlockSpec(memory_space=pltpu.HBM)] * 3,
        out_specs=[vmem()] * (tp_count + 2),
        scratch_shapes=[
            pltpu.VMEM((rows, full), BF16),
            pltpu.VMEM((rows, cols), BF16),
            pltpu.VMEM((1, full), F32),
            pltpu.SemaphoreType.DMA((3,)),
        ],
        compiler_params=params(4),
        name="cut_heads",
    )(me, off_chip(attn_part[0]), off_chip(resid), off_chip(refusal))
    parts = [swap(value, "tp", k + 1) for k, value in enumerate(slices)]

    def load(source, at):
        return pl.pallas_call(
            load_kernel,
            out_shape=pltpu.VMEM((local_experts, 2 * cols, hidden), BF16),
            in_specs=[smem(), pl.BlockSpec(memory_space=pltpu.HBM)],
            out_specs=vmem(),
            scratch_shapes=[pltpu.SemaphoreType.DMA((local_experts,))],
            compiler_params=params(8),
            cost_estimate=pl.CostEstimate(flops=0, bytes_accessed=4 * cols * hidden * local_experts, transcendentals=0),
            name="load_rows",
        )(at, off_chip(source))

    held_gate = load(w_gate, after(me, share))
    base = after(base, held_gate)

    message, projected = pl.pallas_call(
        functools.partial(project_kernel, experts),
        out_shape=[shape(rows, cols + tail), shape(rows, cols, dtype=F32)],
        in_specs=[vmem()] * (5 + tp_count),
        out_specs=[vmem()] * 2,
        compiler_params=params(4),
        name="project",
    )(base, share, unit, norm_gain.reshape(1, cols), route_ids, gate_q, *parts)

    groups = [join(message, swap(message, "tp", 1))]
    bit = 2
    while bit < tp_count:
        groups.append(swap(groups[0] if bit == 2 else join(*groups), "tp", bit))
        bit *= 2
    sizes = [group.shape[0] // rows for group in groups]
    starts = [0] + sizes[1:]

    plane = cross_plane(groups[0], exp_count)
    held_up = load(w_up, after(me, groups[0]))
    groups[1:] = [after(group, held_up) for group in groups[1:]]
    plane = {pattern: after(piece, groups[-1]) if pattern else piece for pattern, piece in plane.items()}

    state, held_down = [], {}
    places = list(reversed(range(tp_count)))
    halves = [(0, local_experts)] if local_experts == 1 else [(0, local_experts // 2), (local_experts // 2, local_experts)]
    units = [(k, low, high) for k in places for low, high in halves]

    def part_of(unit):
        return pltpu.VMEM((unit[2] - unit[1], hidden, cols), BF16)

    for i, group in enumerate(groups):
        if i:
            plane = cross_plane(group, exp_count)
            plane = {pattern: after(piece, state[-1]) for pattern, piece in plane.items()}
        pieces = cross_core(plane)
        chunks, flip = sizes[i], starts[i]
        start, last = i == 0, i == len(groups) - 1
        ahead = units[len(held_down) :][: len(halves)]
        acc = pltpu.VMEM((local_experts, total_rows, hidden), F32)
        held = i == 0 or chunks == sizes[i - 1]
        late = held and i > 0
        refill = held and not late and not last and sizes[i + 1] == chunks
        if last:
            out_shape = [shape(total_rows, local_experts * hidden)]
            out_specs = [pl.BlockSpec((total_rows, hidden), lambda e, *_: (0, e))]
        else:
            out_shape = [acc, acc, pltpu.VMEM((total_rows, tail), F32)]
            out_specs = [vmem()] * 3
        weights = [on_chip(held_gate), on_chip(held_up)] if held else [w_gate, w_up]
        specs = [vmem()] * 2
        if not held:
            specs = [
                pl.BlockSpec(
                    (1, chunks * cols, hidden),
                    lambda e, me, first, flip=flip, chunks=chunks: (e, (me[0] ^ flip) // chunks, 0),
                )
            ] * 2
        aliases = {} if start or last else {7 + len(pieces) + j: j for j in range(3)}
        if held:
            aliases.update({5: len(out_shape), 6: len(out_shape) + 1})
            out_shape += [pltpu.VMEM((local_experts, chunks * cols, hidden), BF16)] * 2
            out_specs += [vmem()] * 2
        found = pl.pallas_call(
            functools.partial(up_kernel, start, last, held, late, refill, chunks, ahead, full, experts),
            out_shape=out_shape + [part_of(unit) for unit in ahead],
            grid_spec=pltpu.PrefetchScalarGridSpec(
                num_scalar_prefetch=2,
                grid=(local_experts,),
                in_specs=[pl.BlockSpec(memory_space=pltpu.HBM)] * 3 + specs + [vmem()] * (len(pieces) + len(state)),
                out_specs=out_specs + [vmem()] * len(ahead),
                scratch_shapes=[pltpu.VMEM((total_rows, chunks * cols), BF16)]
                + ([pltpu.VMEM((total_rows, tail), F32)] if last else [])
                + [pltpu.SemaphoreType.DMA((2 + len(ahead), local_experts))],
            ),
            input_output_aliases=aliases,
            compiler_params=params(small * 3 // 2 if held else 22),
            cost_estimate=pl.CostEstimate(
                flops=4 * total_rows * chunks * cols * hidden * local_experts,
                bytes_accessed=4 * chunks * cols * hidden * local_experts,
                transcendentals=0,
            ),
            name="gate_up",
        )(
            *(me, first, off_chip(w_gate), off_chip(w_up), off_chip(w_down)),
            *weights,
            *pieces,
            *[on_chip(v) for v in state],
        )
        held_down.update(zip(ahead, found[-len(ahead) :]))
        if held:
            held_gate, held_up = found[len(out_shape) - 2 : len(out_shape)]
        state = found[: 1 if last else 3]
    activation = state[0]

    steps = 2 if cols % (2 * LANES) == 0 else 1
    width = cols // steps
    stages = len(orders[0]) + 1
    events = [(0, None)]
    for j in range(1, tp_count):
        events += [(j, None)] + ([(j - 1, 0)] if j < tp_count - 1 else [])
    near = tp_count - 2
    for stage in range(1, stages):
        events += [(j, stage) for j in range(near)]
        events += [(near, 0)] if stage == 1 else []
    events += [(near + 1, 0), (near, stages - 1), (near + 1, stages - 1)]
    mine, theirs, opened, done = {}, {}, [], []
    for j, stage in events:
        k = places[j]
        order = orders[k % 2]
        if stage is None:
            ahead = units[len(held_down) :]
            ahead = ahead[: max(1, sum(unit[0] in places[: j + 2] for unit in ahead))]
            held = [part_of(unit) for unit in ahead]
            parts = [on_chip(held_down[(k, low, high)]) for low, high in halves]
            keep, send, *found = pl.pallas_call(
                functools.partial(down_kernel, relative_order([core] + order), halves, ahead),
                out_shape=[shape(total_rows // 2, cols)] * 2 + held,
                grid_spec=pltpu.PrefetchScalarGridSpec(
                    num_scalar_prefetch=1,
                    grid=(steps,),
                    in_specs=[vmem()] * (1 + len(parts)) + [pl.BlockSpec(memory_space=pltpu.HBM)] * bool(held),
                    out_specs=[pl.BlockSpec((total_rows // 2, width), lambda i, me: (0, i))] * 2 + [vmem()] * len(held),
                    scratch_shapes=[pltpu.SemaphoreType.DMA((len(held), local_experts))] * bool(held),
                ),
                compiler_params=params(2 * small),
                cost_estimate=pl.CostEstimate(
                    flops=2 * total_rows * cols * hidden * local_experts,
                    bytes_accessed=2 * cols * hidden * local_experts,
                    transcendentals=0,
                ),
                name="down",
            )(me, after(activation, *opened[-1:]), *parts, *[off_chip(w_down)] * bool(held))
            held_down.update(zip(ahead, found))
            mine[k], theirs[k] = keep, swap(send, "exp", core)
        elif stage < stages - 1:
            got = after(theirs[k], *opened[-1:])
            if j < near:
                middle = mine[k].shape[0] // 2
                away = [add(mine[k][middle:], got[middle:])]
                mine[k], theirs[k] = add(mine[k][:middle], got[:middle]), swap(away[0], "exp", order[stage])
            else:
                sums = [add(mine[k][i : i + rows], got[i : i + rows]) for i in range(0, got.shape[0], rows)]
                mine[k], away = sums[0], sums[1:]
                theirs[k] = [swap(part, "exp", pattern) for part, pattern in zip(away, relative_order(order)[1:])]
            opened.append(away[-1])
        else:
            last, *others = theirs[k] if j >= near else [theirs[k]]
            parts = [mine[k], after(last, *opened[-1:]), *others]
            if k:
                away = functools.reduce(sum_of, parts).astype(BF16)
                opened.append(away)
                done.append(swap(away, "tp", k))
            else:
                done += parts
    return functools.reduce(sum_of, [projected] + done).astype(BF16)


def solution(mesh):
    return jax.shard_map(
        local,
        mesh=mesh,
        in_specs=(
            P("tp", "exp", None),
            P("exp", "tp"),
            P(),
            P("tp"),
            P("exp", None),
            P("exp", None),
            P("exp", None, "tp"),
            P("exp", None, "tp"),
            P("exp", "tp", None),
        ),
        out_specs=P("exp", "tp"),
        check_vma=False,
    )
```
